256 devices in a mesh: samp: 32 (over z, x_hi, core), var: 8 (over x_lo, y).
Axes of the slice: x: 4 (x_hi: 2, x_lo: 2; x = x_hi * 2 + x_lo), y: 4, z: 8, core: 2. Of those that a mesh axis runs over, the one named last changes fastest.
Arguments:
- genotypes: bfloat16 [34560, 32768], P('samp', 'var'), may hold values from 0 to 2, as said below
- residual: float32 [34560, 256], P('samp'), may hold values from -6 to 6
- coefficients: float32 [256, 32768], P('samp', 'var'), may hold values from -0.06 to 0.06
- penalty: float32 [32768], P('var'), may hold values from 0.2 to 3
- colors: int32 [2, 8], P(None, 'var'), may hold values from 0 to 1
Outputs:
- coefficients_out: float32 [256, 32768], P('samp', 'var')
- residual_out: float32 [34560, 256], P('samp')
The draws below stay inside these ranges and needn't reach their ends.
Inputs may be any that keep to these rules, and one draw needn't show every extreme that they name: `genotypes`: dosages of a genotype, whole numbers. `colors`: entry (r, v) names which of the 2 blocks of group v is updated in round r.
All inputs are finite; a program needn't handle non-finite values.
Results may differ from the reference program's by a relative error of at most 0.014.
Values may be sent and summed in bfloat16 or wider, within the bound.
A program may use at most 64 MiB of HBM per device.

```python
import math
import jax
import jax.numpy as jnp
from jax import lax

K = 256
BS = 2048
NBLK_DEV = 2
ROUNDS = 2
SAMP_DEV = 1080
SAMPLES = 34560
VARIANTS = 32768
N_VAR = 8


def draw_genotypes(key, part):
    freq_key = jax.random.fold_in(key, 11)
    allele_key = jax.random.fold_in(key, 12)
    groups = SAMPLES // SAMP_DEV
    frequency = jax.random.randint(freq_key, (groups, VARIANTS), 5, 51)

    def one_group(group_index):
        draws = jax.random.randint(jax.random.fold_in(allele_key, group_index), (SAMP_DEV, VARIANTS), 0, 10000)
        limit = frequency[group_index][None, :]
        first_allele = (draws % 100 < limit).astype(jnp.int32)
        second_allele = (draws // 100 < limit).astype(jnp.int32)
        return (first_allele + second_allele).astype(jnp.float32).astype(jnp.bfloat16)
    stacked = lax.map(one_group, jnp.arange(groups, dtype=jnp.int32))
    return stacked.reshape(SAMPLES, VARIANTS)


def place_ends(result, own_key, low, largest):
    longest = result.shape.index(max(result.shape))
    spots = []
    for shift in (0, 1):
        where = [jax.random.randint(jax.random.fold_in(own_key, axis), (), 0, length) for axis, length in enumerate(result.shape)]
        where[longest] = (where[longest] + shift) % result.shape[longest]
        spots.append(tuple(where))
    return result.at[spots[0]].set(low).at[spots[1]].set(largest)


def block_scale(rng, dims, pieces, smallest, largest):
    def one(position, shards_of):
        steps = jax.random.uniform(jax.random.fold_in(jax.random.fold_in(rng, 6), position), (shards_of,), jnp.float32, smallest / len(pieces), largest / len(pieces))
        return jnp.repeat(jnp.exp(steps), dims[position] // shards_of).reshape((-1,) + (1,) * (len(dims) - position - 1))

    factor_of = one(*pieces[0])
    for cut in pieces[1:]:
        factor_of = factor_of * one(*cut)
    return factor_of


def bell_draw(stream_key, dims, width, most, cuts=(), held_as=jnp.bfloat16):
    gain = block_scale(stream_key, dims, cuts, -0.22, 0.18) if cuts else 1.0
    array = jax.random.normal(stream_key, dims, jnp.float32) * width * gain
    return jnp.minimum(jnp.maximum(array, -most), most).astype(held_as)


def setup_inputs(seed: int = 0) -> dict:
    splits = jax.random.split(jax.random.key(seed), 6)
    genotypes = draw_genotypes(jax.random.fold_in(splits[5], 71), 0)
    residual = bell_draw(splits[1], (SAMPLES, K), 1.0, 6.0, ((0, 32),), jnp.float32)
    coefficients = bell_draw(splits[2], (K, VARIANTS), 0.01, 0.06, ((0, 32), (1, 8)), jnp.float32)
    penalty = jnp.clip(jnp.exp(math.log(3.0) - 2.7080502 * jax.random.uniform(splits[3], (VARIANTS,), jnp.float32) ** block_scale(splits[3], (VARIANTS,), ((0, 8),), -0.2, 0.2)), 0.2, 3.0)
    colors = place_ends(jax.random.randint(splits[4], (ROUNDS, N_VAR), 0, NBLK_DEV), jax.random.fold_in(splits[4], 1), 0, NBLK_DEV - 1).astype(jnp.int32)
    return dict(genotypes=genotypes, residual=residual, coefficients=coefficients, penalty=penalty, colors=colors)


def column_moments(block_values):
    wide = block_values.astype(jnp.float32)
    counts = lax.optimization_barrier(jnp.sum(wide, axis=0))
    squares = lax.optimization_barrier(jnp.sum(wide * wide, axis=0))
    return (counts, squares)

def reference(genotypes, residual, coefficients, penalty, colors):
    group_width = NBLK_DEV * BS
    for round_index in range(ROUNDS):
        rounded = residual.astype(jnp.bfloat16)
        correction = jnp.zeros(residual.shape, jnp.float32)
        for group_index in range(N_VAR):
            first_column = (group_index * group_width + colors[round_index, group_index] * BS).astype(jnp.int32)
            block_values = lax.dynamic_slice_in_dim(genotypes, first_column, BS, 1)
            counts, squares = column_moments(block_values)
            column_mean = counts / SAMPLES
            column_scale = squares - counts * column_mean
            centered = (block_values.astype(jnp.float32) - column_mean[None, :]).astype(jnp.bfloat16)
            gradient = lax.dot_general(rounded, centered, (((0,), (0,)), ((), ())), preferred_element_type=jnp.float32)
            old_rows = lax.dynamic_slice_in_dim(coefficients, first_column, BS, 1)
            shifted = old_rows + gradient / column_scale[None, :]
            group_norm = jnp.sqrt(lax.optimization_barrier(jnp.sum(shifted * shifted, axis=0)) + 1e-06)
            penalty_part = lax.dynamic_slice_in_dim(penalty, first_column, BS, 0)
            shrink = jnp.maximum(0.0, 1.0 - penalty_part * jnp.sqrt(K / column_scale) / group_norm)
            new_rows = shrink[None, :] * shifted
            coefficients = lax.dynamic_update_slice(coefficients, new_rows, (jnp.int32(0), first_column))
            change_rows = (new_rows - old_rows).astype(jnp.bfloat16)
            correction = correction + lax.dot_general(centered, change_rows, (((1,), (1,)), ((), ())), preferred_element_type=jnp.float32)
        residual = residual - correction
    return (coefficients, residual)
```

```python
import functools

import jax
import jax.numpy as jnp
from jax import lax
from jax.experimental import pallas as pl
from jax.experimental.pallas import tpu as pltpu
from jax.sharding import PartitionSpec as P

K = 256
BS = 2048
ROUNDS = 2
SAMPLES = 34560
ROWS = 1080
PAD = 1152
NS = 32
NT = 16
NV = 8
W = 128
YR = 272
MESH = pl.DeviceIdType.MESH
F32 = jnp.float32
BF16 = jnp.bfloat16


def al(x, m):
    return pl.multiple_of(x, m)


def kernel(
    colors, x_hbm, res_hbm, coef, pen,
    coef_out, res_out,
    xs, tail, rf, rt, rsum, g, st_loc, st_in, st_own, stats, mhl,
    oldb, newb, newt,
    pair_tx, pair_rx, rs_tx, rs_rx, nrm, dmat, c_tx, c_rx, t_buf,
    x_sem, r_sem,
    st_ss, st_rs, sa_ss, sa_rs, old_ss, old_rs, new_ss, new_rs,
    pr_ss, pr_rs, rs_ss, rs_rs, nm_ss, nm_rs, ag_ss, ag_rs, fw_ss, fw_rs,
    cr_ss, cr_rs, ca_ss, ca_rs,
):
    s = lax.axis_index("samp")
    v = lax.axis_index("var")
    t = s // 2
    c = s % 2
    half = s // 16
    partner = s + 1 - 2 * c

    def rcopy(src, dst, ss, rs, samp, var):
        return pltpu.make_async_remote_copy(
            src_ref=src, dst_ref=dst, send_sem=ss, recv_sem=rs,
            device_id=(samp, var), device_id_type=MESH,
        )

    xcopies = []
    for q in range(4):
        xcopies.append(pltpu.make_async_copy(
            x_hbm.at[pl.ds(0, 1072), pl.ds(q * 1024, 1024)],
            xs.at[q // 2, pl.ds(0, 1072), pl.ds(q % 2 * 1024, 1024)], x_sem.at[q]))
        xcopies[-1].start()
    tcopy = pltpu.make_async_copy(x_hbm.at[pl.ds(1072, 8), :], tail, x_sem.at[4])
    tcopy.start()
    rcopy_in = pltpu.make_async_copy(res_hbm, rf.at[pl.ds(0, ROWS), :], r_sem)
    rcopy_in.start()

    barrier = pltpu.get_barrier_semaphore()

    @pl.loop(1, NS)
    def _(i):
        pl.semaphore_signal(barrier, inc=1, device_id=((s + i) % NS, v), device_id_type=MESH)

    @pl.loop(1, NV)
    def _(i):
        pl.semaphore_signal(barrier, inc=1, device_id=(s, (v + i) % NV), device_id_type=MESH)

    rf[pl.ds(ROWS, PAD - ROWS), :] = jnp.zeros((PAD - ROWS, K), F32)
    tcopy.wait()
    for b in range(2):
        xs[b, pl.ds(1088, PAD - 1088), :] = jnp.zeros((PAD - 1088, BS), BF16)
        xs[b, pl.ds(1072, 16), :] = jnp.concatenate(
            [tail[:, pl.ds(b * BS, BS)].astype(F32), jnp.zeros((8, BS), F32)], axis=0).astype(BF16)

    for q in range(4):
        xcopies[q].wait()

        @pl.loop(0, 4)
        def _(u):
            lanes = pl.ds(al(q % 2 * 1024 + u * 256, 256), 256)
            cnt = jnp.zeros((16, 256), F32)
            sqr = jnp.zeros((16, 256), F32)
            for h in range(2):
                b = xs[q // 2, pl.ds(h * 576, 16), lanes]
                a = b
                d = b * b
                for i in range(1, 36):
                    b = xs[q // 2, pl.ds(h * 576 + i * 16, 16), lanes]
                    a = a + b
                    d = d + b * b
                cnt = cnt + a.astype(F32)
                sqr = sqr + d.astype(F32)
            st_loc[q // 2, pl.ds(0, 1), lanes] = jnp.sum(cnt, axis=0, keepdims=True)
            st_loc[q // 2, pl.ds(1, 1), lanes] = jnp.sum(sqr, axis=0, keepdims=True)

    pl.semaphore_wait(barrier, NS - 1 + NV - 1)

    def st_send(p):
        return rcopy(st_loc.at[p // 16, :, pl.ds(al(p % 16 * W, W), W)], st_in.at[s], st_ss.at[p], st_rs.at[s], p, v)

    @pl.loop(1, NS)
    def _(i):
        st_send((s + i) % NS).start()

    st_in[s] = st_loc[half, :, pl.ds(al(s % 16 * W, W), W)]

    def old_send(b, j):
        return (coef.at[:, pl.ds(al(b * BS + j * W, W), W)],
                oldb.at[b, pl.ds(al((s % 16) * 8, 8), 8), :])

    for b in range(2):
        @pl.loop(0, NT)
        def _(i):
            j = (t + i) % NT
            dest = 2 * j + half
            src, dst = old_send(b, j)

            @pl.when(dest != s)
            def _():
                rcopy(src, dst, old_ss.at[b, j], old_rs.at[b, s % 16], dest, v).start()

            @pl.when(dest == s)
            def _():
                oldb[b, pl.ds(al((s % 16) * 8, 8), 8), :] = coef[:, pl.ds(al(b * BS + j * W, W), W)]

    def transposed():
        for i in range(PAD // W):
            rt[:, pl.ds(i * W, W)] = rf[pl.ds(i * W, W), :].T.astype(BF16)
        rsum[...] = jnp.broadcast_to(
            jnp.sum(rt[...].astype(F32), axis=1, keepdims=True), (K, W))

    def products(color):
        @pl.loop(0, 8)
        def _(u):
            lanes = pl.ds(al(u * 256, 256), 256)
            g[:, lanes] = jnp.dot(rt[...], xs[color, :, lanes], preferred_element_type=F32)

    oldb[2] = jnp.zeros((W, W), F32)
    for b in range(2):
        newt[2 + b] = coef[:, pl.ds(b * BS, BS)]
    rcopy_in.wait()
    transposed()
    products(colors[0, 0])

    @pl.loop(1, NS)
    def _(i):
        p = (s + i) % NS
        rcopy(st_loc.at[0, :, pl.ds(0, W)], st_in.at[p], st_ss.at[p], st_rs.at[p], p, v).wait_recv()

    total = jnp.sum(st_in[...], axis=0)
    mean_own = total[0:1] / SAMPLES
    st_own[pl.ds(0, 1), :] = mean_own
    st_own[pl.ds(1, 1), :] = total[1:2] - total[0:1] * mean_own

    def sa_send(p):
        return rcopy(st_own, stats.at[half, :, pl.ds(al(s % 16 * W, W), W)], sa_ss.at[p], sa_rs.at[s], p, v)

    @pl.loop(1, NS)
    def _(i):
        sa_send((s + i) % NS).start()

    stats[half, :, pl.ds(al(s % 16 * W, W), W)] = st_own[...]

    @pl.loop(1, NS)
    def _(i):
        p = (s + i) % NS
        rcopy(st_own, stats.at[p // 16, :, pl.ds(al(p % 16 * W, W), W)], sa_ss.at[p], sa_rs.at[p], p, v).wait_recv()

    for b in range(2):
        mean_all = stats[b, pl.ds(0, 1), :]
        high = mean_all.astype(BF16).astype(F32)
        mhl[b] = jnp.concatenate(
            [jnp.broadcast_to(high, (8, BS)), jnp.broadcast_to(mean_all - high, (8, BS))],
            axis=0).astype(BF16)

    own_rows = pl.ds(al(c * W, W), W)
    other_rows = pl.ds(al((1 - c) * W, W), W)
    own_lanes = pl.ds(al(t * W, W), W)

    def new_copy(r, i):
        return (newb.at[r, pl.ds(al(i * 8, 8), 8), :], newt.at[r, :, own_lanes])

    for r in range(ROUNDS):
        color = colors[r, 0]
        if r > 0:
            transposed()
            products(color)

        def pair_copy(u):
            lanes = pl.ds(al(u * 512, 512), 512)
            return rcopy(pair_tx.at[r, :, lanes], pair_rx.at[r, :, lanes],
                         pr_ss.at[r, u], pr_rs.at[r, u], partner, v)

        @pl.loop(0, 4)
        def _(u):
            lanes = pl.ds(al(u * 512, 512), 512)
            mean = stats[color, pl.ds(0, 1), lanes]
            rs_o = rsum[other_rows, :][:, 0:1]
            pair_tx[r, :, lanes] = (g[other_rows, lanes] - rs_o * mean).astype(BF16)
            pair_copy(u).start()

        def rs_copy(j, i_src):
            return rcopy(rs_tx.at[r, j], rs_rx.at[r, i_src], rs_ss.at[r, j], rs_rs.at[r, i_src], 2 * j + c, v)

        @pl.loop(0, 4)
        def _(u):
            lanes = pl.ds(al(u * 512, 512), 512)
            mean = stats[color, pl.ds(0, 1), lanes]
            rs_o = rsum[own_rows, :][:, 0:1]
            mine = g[own_rows, lanes] - rs_o * mean
            pair_copy(u).wait_recv()
            mine = mine + pair_rx[r, :, lanes].astype(F32)
            g[own_rows, lanes] = mine
            low = mine.astype(BF16)
            for w in range(4):
                rs_tx[r, u * 4 + w] = low[:, w * W:(w + 1) * W]
            for w in range(4):
                j = u * 4 + w

                @pl.when(j != t)
                def _():
                    rs_copy(j, t).start()

        newb[r] = g[own_rows, own_lanes]

        @pl.loop(1, NT)
        def _(i):
            j = (t + i) % NT
            rs_copy(j, j).wait_recv()
            newb[r] = newb[r] + rs_rx[r, j].astype(F32)

        if r == 0:
            for b in range(2):
                @pl.loop(0, 16)
                def _(i):
                    src_dev = 16 * c + i

                    @pl.when(src_dev != s)
                    def _():
                        rcopy(coef.at[:, pl.ds(0, W)], oldb.at[b, pl.ds(al(i * 8, 8), 8), :],
                              old_ss.at[b, i], old_rs.at[b, i], src_dev, v).wait_recv()
            old = oldb[color]
        else:
            gap = color - colors[0, 0]
            old = oldb[color + (1 - gap * gap) * (2 - color)]
        scale = stats[color, pl.ds(1, 1), own_lanes]
        shifted = old + newb[r] / scale
        part = jnp.sum(shifted * shifted, axis=0, keepdims=True)
        nrm[r, 0] = jnp.broadcast_to(part, (8, W))
        ncopy = rcopy(nrm.at[r, 0], nrm.at[r, 1], nm_ss.at[r], nm_rs.at[r], partner, v)
        ncopy.start()
        push = pen[color, :, own_lanes] * jnp.sqrt(K / scale)
        ncopy.wait_recv()
        norm = jnp.sqrt(part + nrm[r, 1][0:1] + 1e-06)
        new = jnp.maximum(0.0, 1.0 - push / norm) * shifted
        dmat[r, own_rows, own_lanes] = (new - old).astype(BF16)
        newb[r] = new
        if r == 0:
            oldb[2] = new

        def d_view(core, j):
            return dmat.at[r, pl.ds(al(core * W, W), W), pl.ds(al(j * W, W), W)]

        def ag_copy(j, i_src):
            return rcopy(d_view(c, i_src), d_view(c, i_src), ag_ss.at[r, j], ag_rs.at[r, i_src], 2 * j + c, v)

        def fw_copy(core, j):
            return rcopy(d_view(core, j), d_view(core, j), fw_ss.at[r, j], fw_rs.at[r, j], partner, v)

        @pl.loop(1, NT)
        def _(i):
            ag_copy((t + i) % NT, t).start()

        fw_copy(c, t).start()

        @pl.loop(0, 16)
        def _(i):
            dest = 16 * c + i
            src, dst = new_copy(r, i)

            @pl.when(dest != s)
            def _():
                rcopy(src, dst, new_ss.at[r, i], new_rs.at[r, t], dest, v).start()

            @pl.when(dest == s)
            def _():
                newt[r, :, own_lanes] = newb[r, pl.ds(al(i * 8, 8), 8), :]

        @pl.loop(1, NT)
        def _(i):
            j = (t + i) % NT
            ag_copy(j, j).wait_recv()
            fw_copy(c, j).start()

        @pl.loop(0, NT)
        def _(i):
            fw_copy(1 - c, (t + i) % NT).wait_recv()

        nt = (((1,), (1,)), ((), ()))
        md = lax.dot_general(mhl[color], dmat[r], nt, preferred_element_type=F32)
        md = md[0:1] + md[8:9]
        yv = v % 4
        xv = v // 4

        def cr_copy(p):
            return rcopy(c_tx.at[r, p], c_rx.at[r, v], cr_ss.at[r, p], cr_rs.at[r, v], p_samp, p)

        p_samp = s

        @pl.loop(0, 4)
        def _(i):
            y = (yv + 1 + i) % 4
            out = lax.dot_general(xs[color, pl.ds(al(y * YR, 16), YR), :], dmat[r], nt,
                                  preferred_element_type=F32) - md
            for w in range(2):
                c_tx[r, w * 4 + y] = out[:, w * W:(w + 1) * W].astype(BF16)
            for w in range(2):
                p = w * 4 + y

                @pl.when(p != v)
                def _():
                    cr_copy(p).start()

        def cr_recv(p):
            return rcopy(c_tx.at[r, p], c_rx.at[r, p], cr_ss.at[r, p], cr_rs.at[r, p], s, p)

        g[pl.ds(0, 256), pl.ds(0, W)] = c_tx[r, v, pl.ds(0, 256), :].astype(F32)
        g[pl.ds(0, 16), pl.ds(W, W)] = c_tx[r, v, pl.ds(256, 16), :].astype(F32)

        @pl.loop(1, NV)
        def _(i):
            p = (v + i) % NV
            cr_recv(p).wait_recv()
            g[pl.ds(0, 256), pl.ds(0, W)] += c_rx[r, p, pl.ds(0, 256), :].astype(F32)
            g[pl.ds(0, 16), pl.ds(W, W)] += c_rx[r, p, pl.ds(256, 16), :].astype(F32)

        t_buf[r, v, pl.ds(0, 256), :] = g[pl.ds(0, 256), pl.ds(0, W)].astype(BF16)
        t_buf[r, v, pl.ds(256, 16), :] = g[pl.ds(0, 16), pl.ds(W, W)].astype(BF16)

        def ca_copy(p, i_src):
            return rcopy(t_buf.at[r, i_src], t_buf.at[r, i_src], ca_ss.at[r, p], ca_rs.at[r, i_src], s, p)

        @pl.loop(1, NV)
        def _(i):
            ca_copy((v + i) % NV, v).start()

        def subtract(p):
            for w in range(2):
                @pl.when(p // 4 == w)
                def _():
                    rows = pl.ds(al((p % 4) * YR, 16), YR)
                    lanes = pl.ds(w * W, W)
                    rf[rows, lanes] = rf[rows, lanes] - t_buf[r, p].astype(F32)

        subtract(v)

        @pl.loop(1, NV)
        def _(i):
            p = (v + i) % NV
            ca_copy(p, p).wait_recv()
            subtract(p)

        rf[pl.ds(ROWS, 8), :] = jnp.zeros((8, K), F32)

    res_out[...] = rf[pl.ds(0, ROWS), :]

    for r in range(ROUNDS):
        @pl.loop(0, NT)
        def _(i):
            @pl.when(2 * i + half != s)
            def _():
                rcopy(newb.at[r, pl.ds(0, 8), :], newt.at[r, :, pl.ds(al(i * W, W), W)],
                      new_ss.at[r, i], new_rs.at[r, i], 2 * i + half, v).wait_recv()

    for b in range(2):
        lanes = pl.ds(b * BS, BS)
        d0 = colors[0, 0] - b
        d1 = colors[1, 0] - b
        coef_out[:, lanes] = newt[1 - d1 * d1 + d1 * d1 * d0 * d0 * (2 + b)]

    @pl.loop(1, NS)
    def _(i):
        p = (s + i) % NS
        st_send(p).wait_send()
        sa_send(p).wait_send()

    for b in range(2):
        @pl.loop(0, NT)
        def _(j):
            @pl.when(2 * j + half != s)
            def _():
                src, dst = old_send(b, j)
                rcopy(src, dst, old_ss.at[b, j], old_rs.at[b, s % 16], 2 * j + half, v).wait_send()

    for r in range(ROUNDS):
        @pl.loop(0, 4)
        def _(u):
            lanes = pl.ds(al(u * 512, 512), 512)
            rcopy(pair_tx.at[r, :, lanes], pair_rx.at[r, :, lanes],
                  pr_ss.at[r, u], pr_rs.at[r, u], partner, v).wait_send()

        rcopy(nrm.at[r, 0], nrm.at[r, 1], nm_ss.at[r], nm_rs.at[r], partner, v).wait_send()

        @pl.loop(0, 16)
        def _(i):
            @pl.when(16 * c + i != s)
            def _():
                src, dst = new_copy(r, i)
                rcopy(src, dst, new_ss.at[r, i], new_rs.at[r, t], 16 * c + i, v).wait_send()

        @pl.loop(0, NT)
        def _(j):
            view = dmat.at[r, own_rows, pl.ds(al(j * W, W), W)]
            rcopy(view, view, fw_ss.at[r, j], fw_rs.at[r, j], partner, v).wait_send()

            @pl.when(j != t)
            def _():
                rcopy(rs_tx.at[r, j], rs_rx.at[r, t], rs_ss.at[r, j], rs_rs.at[r, t], 2 * j + c, v).wait_send()
                mine = dmat.at[r, own_rows, own_lanes]
                rcopy(mine, mine, ag_ss.at[r, j], ag_rs.at[r, t], 2 * j + c, v).wait_send()

        @pl.loop(1, NV)
        def _(i):
            p = (v + i) % NV
            rcopy(c_tx.at[r, p], c_rx.at[r, v], cr_ss.at[r, p], cr_rs.at[r, v], s, p).wait_send()
            rcopy(t_buf.at[r, v], t_buf.at[r, v], ca_ss.at[r, p], ca_rs.at[r, v], s, p).wait_send()


def shards(genotypes, residual, coefficients, penalty, colors):
    dma = pltpu.SemaphoreType.DMA
    vm = pltpu.VMEM
    coef, res = pl.pallas_call(
        kernel,
        out_shape=(jax.ShapeDtypeStruct((8, 2 * BS), F32), jax.ShapeDtypeStruct((ROWS, K), F32)),
        in_specs=[
            pl.BlockSpec(memory_space=pltpu.SMEM),
            pl.BlockSpec(memory_space=pl.ANY),
            pl.BlockSpec(memory_space=pl.ANY),
            pl.BlockSpec(memory_space=pltpu.VMEM),
            pl.BlockSpec(memory_space=pltpu.VMEM),
        ],
        out_specs=[pl.BlockSpec(memory_space=pltpu.VMEM)] * 2,
        scratch_shapes=[
            vm((2, PAD, BS), BF16), vm((8, 2 * BS), BF16), vm((PAD, K), F32), vm((K, PAD), BF16),
            vm((K, W), F32), vm((K, BS), F32), vm((2, 2, BS), F32), vm((NS, 2, W), F32),
            vm((2, W), F32), vm((2, 2, BS), F32), vm((2, 16, BS), BF16),
            vm((3, W, W), F32), vm((2, W, W), F32), vm((4, 8, BS), F32),
            vm((2, W, BS), BF16), vm((2, W, BS), BF16),
            vm((2, NT, W, W), BF16), vm((2, NT, W, W), BF16), vm((2, 2, 8, W), F32),
            vm((2, K, BS), BF16),
            vm((2, NV, YR, W), BF16), vm((2, NV, YR, W), BF16), vm((2, NV, YR, W), BF16),
            dma((5,)), dma,
            dma((NS,)), dma((NS,)), dma((NS,)), dma((NS,)),
            dma((2, 16)), dma((2, 16)), dma((2, 16)), dma((2, 16)),
            dma((2, 4)), dma((2, 4)), dma((2, NT)), dma((2, NT)), dma((2,)), dma((2,)),
            dma((2, NT)), dma((2, NT)), dma((2, NT)), dma((2, NT)),
            dma((2, NV)), dma((2, NV)), dma((2, NV)), dma((2, NV)),
        ],
        compiler_params=pltpu.CompilerParams(
            collective_id=0, has_side_effects=True, vmem_limit_bytes=56 * 1024 * 1024),
    )(colors, genotypes, residual, coefficients, penalty.reshape(2, 1, BS))
    return (coef, res)


def solution(mesh):
    placed = (P("samp", "var"), P("samp", None), P("samp", "var"), P("var"), P(None, "var"))
    return jax.shard_map(
        shards,
        mesh=mesh,
        in_specs=placed,
        out_specs=(P("samp", "var"), P("samp", None)),
        check_vma=False,
    )
```

```python
import jax
import jax.numpy as jnp
from jax import lax
from jax.experimental import pallas as pl
from jax.experimental.pallas import tpu as pltpu
from jax.sharding import PartitionSpec as P

K = 256
BS = 2048
ROUNDS = 2
SAMPLES = 34560
ROWS = 1080
PAD = 1152
NS = 32
NT = 16
NV = 8
W = 128
HW = 64
YR = 272
PR = 136
MESH = pl.DeviceIdType.MESH
F32 = jnp.float32
BF16 = jnp.bfloat16
NN_T = (((1,), (1,)), ((), ()))


def al(x, m):
    return pl.multiple_of(x, m)


def zigzag(a, middle):
    return middle + (1 - 2 * (a % 2)) * ((a + 1) // 2)


def split(x):
    high = x.astype(BF16).astype(F32)
    return high, x - high


def kernel(
    colors, x_hbm, res_hbm, coef, pen,
    coef_out, res_out,
    xs, tail, rf, rt, rsum, g, gacc, st_loc, st_in, rg_loc, rg_in, fix, mean_own, scale_own, means, mhl,
    cb, stage, oldr, pick, newb, newt,
    pair_tx, pair_rx, rs_tx, rs_rx, nrm, dmat, c_tx, c_rx, t_buf, tacc,
    x_sem, r_sem,
    st_ss, st_rs, rg_ss, rg_rs, mn_ss, mn_rs, old_ss, old_rs, new_ss, new_rs,
    pr_ss, pr_rs, rs_ss, rs_rs, nm_ss, nm_rs, ag_ss, ag_rs, fw_ss, fw_rs,
    cr_ss, cr_rs, ca_ss, ca_rs,
):
    s = lax.axis_index("samp")
    v = lax.axis_index("var")
    t = s // 2
    c = s % 2
    z = s // 4
    xh = t % 2
    yv = v % 4
    xv = v // 4
    partner = s + 1 - 2 * c
    holder = (s // 8) % 2
    place = pl.ds(al((s // 16) * HW + (s % 8) * 8, 8), 8)
    own_lanes = pl.ds(al(t * W, W), W)

    def chip(i):
        return ((z + zigzag(i // 2, 4)) % 8) * 2 + (xh + 1 - i % 2) % 2

    def group(i):
        return ((xv + 1 - i % 2) % 2) * 4 + (yv + zigzag(i // 2, 2)) % 4

    def rcopy(src, dst, ss, rs, samp, var):
        return pltpu.make_async_remote_copy(
            src_ref=src, dst_ref=dst, send_sem=ss, recv_sem=rs,
            device_id=(samp, var), device_id_type=MESH,
        )

    xcopies = []
    for q in range(4):
        xcopies.append(pltpu.make_async_copy(
            x_hbm.at[pl.ds(0, 1072), pl.ds(q * 1024, 1024)],
            xs.at[q // 2, pl.ds(0, 1072), pl.ds(q % 2 * 1024, 1024)], x_sem.at[q]))
    tcopy = pltpu.make_async_copy(x_hbm.at[pl.ds(1072, 8), :], tail, x_sem.at[4])
    rcopy_in = pltpu.make_async_copy(res_hbm, rf.at[pl.ds(0, ROWS), :], r_sem)
    rcopy_in.start()
    tcopy.start()
    for q in range(4):
        xcopies[q].start()

    barrier = pltpu.get_barrier_semaphore()

    @pl.loop(1, NS)
    def _(i):
        pl.semaphore_signal(barrier, inc=1, device_id=((s + i) % NS, v), device_id_type=MESH)

    @pl.loop(1, NV)
    def _(i):
        pl.semaphore_signal(barrier, inc=1, device_id=(s, (v + i) % NV), device_id_type=MESH)

    for b in range(2):
        cb[b] = coef[:, pl.ds(b * BS, BS)]
        newt[2 + b] = coef[:, pl.ds(b * BS, BS)]
    for r in range(ROUNDS):
        stage[r] = cb[colors[0, r]]

    def transposed(h):
        rows = pl.ds(h * W, W)
        for i in range(PAD // W):
            rt[rows, pl.ds(i * W, W)] = rf[pl.ds(i * W, W), pl.ds(h * W, W)].T.astype(BF16)
        rsum[rows, :] = jnp.broadcast_to(
            jnp.sum(rt[rows, :].astype(F32), axis=1, keepdims=True), (W, W))

    rf[pl.ds(ROWS, PAD - ROWS), :] = jnp.zeros((PAD - ROWS, K), F32)
    rcopy_in.wait()
    transposed(0)
    transposed(1)
    for h in range(2):
        rg_loc[pl.ds(h, 1), :] = jnp.sum(
            rf[:, pl.ds(h * W, W)].astype(BF16).astype(F32), axis=0, keepdims=True)
    tcopy.wait()
    for b in range(2):
        xs[b, pl.ds(1088, PAD - 1088), :] = jnp.zeros((PAD - 1088, BS), BF16)
        xs[b, pl.ds(1072, 16), :] = jnp.concatenate(
            [tail[:, pl.ds(b * BS, BS)].astype(F32), jnp.zeros((8, BS), F32)], axis=0).astype(BF16)

    for q in range(4):
        xcopies[q].wait()

        @pl.loop(0, 4)
        def _(u):
            lanes = pl.ds(al(q % 2 * 1024 + u * 256, 256), 256)
            cnt = jnp.zeros((16, 256), F32)
            sqr = jnp.zeros((16, 256), F32)
            for h in range(2):
                b = xs[q // 2, pl.ds(h * 576, 16), lanes]
                a = b
                d = b * b
                for i in range(1, 36):
                    b = xs[q // 2, pl.ds(h * 576 + i * 16, 16), lanes]
                    a = a + b
                    d = d + b * b
                cnt = cnt + a.astype(F32)
                sqr = sqr + d.astype(F32)
            st_loc[q // 2, pl.ds(0, 1), lanes] = jnp.sum(cnt, axis=0, keepdims=True)
            st_loc[q // 2, pl.ds(1, 1), lanes] = jnp.sum(sqr, axis=0, keepdims=True)

    pl.semaphore_wait(barrier, NS - 1 + NV - 1)

    def st_copy(p, i_src):
        return rcopy(st_loc.at[:, :, pl.ds(al(p // 2 * W, W), W)], st_in.at[:, i_src],
                     st_ss.at[p], st_rs.at[i_src], p, v)

    def rg_copy(p, i_src):
        return rcopy(rg_loc, rg_in.at[i_src], rg_ss.at[p], rg_rs.at[i_src], p, v)

    @pl.loop(1, NS)
    def _(i):
        p = (s + i) % NS
        st_copy(p, s).start()
        rg_copy(p, s).start()

    st_in[:, s] = st_loc[:, :, own_lanes]
    rg_in[s] = rg_loc[...]

    def old_copy(r, j):
        return rcopy(stage.at[r, :, pl.ds(al(j * W, W), W)], oldr.at[r, place, :],
                     old_ss.at[r, j], old_rs.at[r, (s // 16) * 8 + s % 8], 2 * j + holder, v)

    def old_sends(r):
        @pl.loop(0, NT)
        def _(j):
            @pl.when(2 * j + holder != s)
            def _():
                old_copy(r, j).start()

            @pl.when(2 * j + holder == s)
            def _():
                oldr[r, place, :] = stage[r, :, pl.ds(al(j * W, W), W)]

    def old_drain(r):
        @pl.loop(0, NT)
        def _(j):
            @pl.when(2 * j + holder != s)
            def _():
                old_copy(r, j).wait_send()

    def sharer(i):
        return (i // 8) * 16 + c * 8 + i % 8

    def old_wait(r):
        @pl.loop(0, 16)
        def _(i):
            @pl.when(sharer(i) != s)
            def _():
                rcopy(stage.at[r, :, pl.ds(0, W)], oldr.at[r, pl.ds(al(i * 8, 8), 8), :],
                      old_ss.at[r, 0], old_rs.at[r, i], sharer(i), v).wait_recv()

    def new_copy(r, i):
        return rcopy(newb.at[r, pl.ds(al(i * 8, 8), 8), :], newt.at[r, :, own_lanes],
                     new_ss.at[r, i], new_rs.at[r, t], sharer(i), v)

    old_sends(0)

    def own_rows(h):
        return pl.ds(al(c * HW, HW), HW)

    def products(r, h):
        @pl.loop(0, 8)
        def _(u):
            lanes = pl.ds(al(u * 256, 256), 256)
            g[h, :, lanes] = jnp.dot(
                rt[pl.ds(h * W, W), :], xs[colors[0, r], :, lanes], preferred_element_type=F32)

    def centre(r, lanes):
        if r == 0:
            return st_loc[colors[0, r], pl.ds(0, 1), lanes] * (1.0 / ROWS)
        return means[colors[0, r], :, lanes]

    def pair_copy(r, h, u):
        lanes = pl.ds(al(u * 1024, 1024), 1024)
        return rcopy(pair_tx.at[r, h, :, lanes], pair_rx.at[r, h, :, lanes],
                     pr_ss.at[r, h, u], pr_rs.at[r, h, u], partner, v)

    def pair_sends(r, h):
        rows = pl.ds(al((1 - c) * HW, HW), HW)
        for u in range(2):
            for w in range(2):
                lanes = pl.ds(u * 1024 + w * 512, 512)
                rs_o = rsum[pl.ds(al(h * W + (1 - c) * HW, HW), HW), :][:, 0:1]
                pair_tx[r, h, :, lanes] = (g[h, rows, lanes] - rs_o * centre(r, lanes)).astype(BF16)
            pair_copy(r, h, u).start()

    def rs_copy(r, h, j, i_src):
        return rcopy(rs_tx.at[r, h, j], rs_rx.at[r, h, i_src], rs_ss.at[r, h, j], rs_rs.at[r, h, i_src],
                     2 * j + c, v)

    def rs_sends(r, h):
        rows = own_rows(h)
        for u in range(2):
            pair_copy(r, h, u).wait_recv()
            for w in range(2):
                lanes = pl.ds(u * 1024 + w * 512, 512)
                rs_o = rsum[pl.ds(al(h * W + c * HW, HW), HW), :][:, 0:1]
                mine = g[h, rows, lanes] - rs_o * centre(r, lanes) + pair_rx[r, h, :, lanes].astype(F32)
                g[h, rows, lanes] = mine
                low = mine.astype(BF16)
                for e in range(4):
                    rs_tx[r, h, u * 8 + w * 4 + e] = low[:, e * W:(e + 1) * W]

        @pl.loop(0, NT - 1)
        def _(i):
            rs_copy(r, h, chip(i), t).start()

    products(0, 0)
    pair_sends(0, 0)
    products(0, 1)
    pair_sends(0, 1)
    rs_sends(0, 0)
    rs_sends(0, 1)

    @pl.loop(1, NS)
    def _(i):
        p = (s + i) % NS
        st_copy(p, p).wait_recv()
        rg_copy(p, p).wait_recv()

    for b in range(2):
        total = jnp.sum(st_in[b], axis=0)
        mean = total[0:1] / SAMPLES
        mean_own[b] = mean
        means[b, :, own_lanes] = mean
        scale_own[b] = total[1:2] - total[0:1] * mean

    def mn_copy(j, i_src):
        return rcopy(mean_own, means.at[:, :, pl.ds(al(i_src * W, W), W)], mn_ss.at[j], mn_rs.at[i_src],
                     2 * j + c, v)

    @pl.loop(0, NT - 1)
    def _(i):
        mn_copy(chip(i), t).start()

    b_high, b_low = split(st_in[colors[0, 0]][:, 0, :] * (1.0 / ROWS) - mean_own[colors[0, 0]])
    right = jnp.concatenate([b_high, b_low, b_high, b_low], axis=0).astype(BF16)
    for h in range(2):
        a_high, a_low = split(rg_in[:, h, :])
        left = jnp.concatenate([a_high, a_high, a_low, a_low], axis=0)
        fix[h] = jnp.dot(left.T.astype(BF16), right, preferred_element_type=F32)

    for r in range(ROUNDS):
        color = colors[0, r]

        for h in range(2):
            rows = pl.ds(h * HW, HW)
            if r == 0:
                gacc[rows, :] = g[h, own_rows(h), own_lanes] + fix[h, own_rows(h), :]
            else:
                gacc[rows, :] = g[h, own_rows(h), own_lanes]

            @pl.loop(0, NT - 1)
            def _(i):
                j = chip(i)
                rs_copy(r, h, j, j).wait_recv()
                gacc[rows, :] = gacc[rows, :] + rs_rx[r, h, j].astype(F32)

        old_wait(r)
        if r == 0:
            old = oldr[0]
        else:
            pick[0] = oldr[1]
            gap = color - colors[0, 0]
            old = pick[1 - gap * gap]
        scale = scale_own[color]
        shifted = old + gacc[...] / scale
        part = jnp.sum(shifted * shifted, axis=0, keepdims=True)
        nrm[r, 0] = jnp.broadcast_to(part, (8, W))
        ncopy = rcopy(nrm.at[r, 0], nrm.at[r, 1], nm_ss.at[r], nm_rs.at[r], partner, v)
        ncopy.start()
        push = pen[color, :, own_lanes] * jnp.sqrt(K / scale)
        ncopy.wait_recv()
        norm = jnp.sqrt(part + nrm[r, 1][0:1] + 1e-06)
        new = jnp.maximum(0.0, 1.0 - push / norm) * shifted
        change = (new - old).astype(BF16)
        for h in range(2):
            dmat[r, pl.ds(al(h * W + c * HW, HW), HW), own_lanes] = change[h * HW:(h + 1) * HW]
        newb[r] = new
        if r == 0:
            pick[1] = new

        def d_view(h, core, j):
            return dmat.at[r, pl.ds(al(h * W + core * HW, HW), HW), pl.ds(al(j * W, W), W)]

        def ag_copy(h, j, i_src):
            return rcopy(d_view(h, c, i_src), d_view(h, c, i_src), ag_ss.at[r, h, j], ag_rs.at[r, h, i_src],
                         2 * j + c, v)

        def fw_copy(h, core, j):
            return rcopy(d_view(h, core, j), d_view(h, core, j), fw_ss.at[r, h, j], fw_rs.at[r, h, j],
                         partner, v)

        for h in range(2):
            @pl.loop(0, NT - 1)
            def _(i):
                ag_copy(h, chip(i), t).start()

            fw_copy(h, c, t).start()

        if r == 0:
            @pl.loop(1, NS)
            def _(i):
                p = (s + i) % NS
                st_copy(p, s).wait_send()
                rg_copy(p, s).wait_send()

            old_drain(0)

            @pl.loop(0, NT - 1)
            def _(i):
                j = chip(i)
                mn_copy(j, j).wait_recv()
                mn_copy(j, t).wait_send()

            for b in range(2):
                high, low = split(means[b])
                mhl[b] = jnp.concatenate(
                    [jnp.broadcast_to(high, (8, BS)), jnp.broadcast_to(low, (8, BS))], axis=0).astype(BF16)
        ncopy.wait_send()
        for h in range(2):
            for u in range(2):
                pair_copy(r, h, u).wait_send()

            @pl.loop(0, NT - 1)
            def _(i):
                rs_copy(r, h, chip(i), t).wait_send()

        def cr_copy(h, p, i_src):
            return rcopy(c_tx.at[r, h, p], c_rx.at[r, h, i_src], cr_ss.at[r, h, p], cr_rs.at[r, h, i_src], s, p)

        for h in range(2):
            @pl.loop(0, NT - 1)
            def _(i):
                j = chip(i)
                ag_copy(h, j, j).wait_recv()
                fw_copy(h, c, j).start()

            @pl.loop(0, NT)
            def _(i):
                fw_copy(h, 1 - c, chip(i)).wait_recv()

            rows = pl.ds(h * W, W)
            md = lax.dot_general(mhl[color], dmat[r, rows, :], NN_T, preferred_element_type=F32)
            md = md[0:1] + md[8:9]

            @pl.loop(0, 4)
            def _(i):
                y = (yv + zigzag(i, 2)) % 4
                out = lax.dot_general(xs[color, pl.ds(al(y * YR, 16), YR), :], dmat[r, rows, :], NN_T,
                                      preferred_element_type=F32) - md
                for w in range(2):
                    c_tx[r, h, w * 4 + y] = out[w * PR:(w + 1) * PR].astype(BF16)
                for w in range(2):
                    p = w * 4 + y

                    @pl.when(p != v)
                    def _():
                        cr_copy(h, p, v).start()

        @pl.loop(0, 16)
        def _(i):
            @pl.when(sharer(i) != s)
            def _():
                new_copy(r, i).start()

            @pl.when(sharer(i) == s)
            def _():
                newt[r, :, own_lanes] = newb[r, pl.ds(al(i * 8, 8), 8), :]

        if r == 0:
            old_sends(1)

        def ca_copy(h, p, i_src):
            return rcopy(t_buf.at[r, h, i_src], t_buf.at[r, h, i_src], ca_ss.at[r, h, p], ca_rs.at[r, h, i_src],
                         s, p)

        for h in range(2):
            tacc[...] = c_tx[r, h, v].astype(F32)

            @pl.loop(0, NV - 1)
            def _(i):
                p = group(i)
                cr_copy(h, p, p).wait_recv()
                tacc[...] = tacc[...] + c_rx[r, h, p].astype(F32)

            t_buf[r, h, v] = tacc[...].astype(BF16)

            @pl.loop(0, NV - 1)
            def _(i):
                ca_copy(h, group(i), v).start()

        for h in range(2):
            @pl.loop(0, NT - 1)
            def _(i):
                ag_copy(h, chip(i), t).wait_send()

            @pl.loop(0, NT)
            def _(i):
                fw_copy(h, c, chip(i)).wait_send()

            @pl.loop(0, NV - 1)
            def _(i):
                cr_copy(h, group(i), v).wait_send()

        for h in range(2):
            lanes = pl.ds(h * W, W)

            def subtract(p):
                rows = pl.ds(al((p % 4) * YR + (p // 4) * PR, 8), PR)
                rf[rows, lanes] = rf[rows, lanes] - t_buf[r, h, p].astype(F32)

            subtract(v)

            @pl.loop(0, NV - 1)
            def _(i):
                p = group(i)
                ca_copy(h, p, p).wait_recv()
                subtract(p)

            if r == 0:
                rf[pl.ds(ROWS, 8), lanes] = jnp.zeros((8, W), F32)
                transposed(h)
                products(1, h)
                pair_sends(1, h)
                rs_sends(1, h)
            else:
                res_out[:, lanes] = rf[pl.ds(0, ROWS), lanes]

    for r in range(ROUNDS):
        @pl.loop(0, NT)
        def _(j):
            @pl.when(2 * j + holder != s)
            def _():
                rcopy(newb.at[r, pl.ds(0, 8), :], newt.at[r, :, pl.ds(al(j * W, W), W)],
                      new_ss.at[r, 0], new_rs.at[r, j], 2 * j + holder, v).wait_recv()

    for b in range(2):
        d0 = colors[0, 0] - b
        d1 = colors[0, 1] - b
        coef_out[:, pl.ds(b * BS, BS)] = newt[1 - d1 * d1 + d1 * d1 * d0 * d0 * (2 + b)]

    old_drain(1)
    for r in range(ROUNDS):
        @pl.loop(0, 16)
        def _(i):
            @pl.when(sharer(i) != s)
            def _():
                new_copy(r, i).wait_send()

        for h in range(2):
            @pl.loop(0, NV - 1)
            def _(i):
                p = group(i)
                rcopy(t_buf.at[r, h, v], t_buf.at[r, h, v], ca_ss.at[r, h, p], ca_rs.at[r, h, v],
                      s, p).wait_send()


def shards(genotypes, residual, coefficients, penalty, colors):
    dma = pltpu.SemaphoreType.DMA
    vm = pltpu.VMEM
    coef, res = pl.pallas_call(
        kernel,
        out_shape=(jax.ShapeDtypeStruct((8, 2 * BS), F32), jax.ShapeDtypeStruct((ROWS, K), F32)),
        in_specs=[
            pl.BlockSpec(memory_space=pltpu.SMEM),
            pl.BlockSpec(memory_space=pl.ANY),
            pl.BlockSpec(memory_space=pl.ANY),
            pl.BlockSpec(memory_space=pltpu.VMEM),
            pl.BlockSpec(memory_space=pltpu.VMEM),
        ],
        out_specs=[pl.BlockSpec(memory_space=pltpu.VMEM)] * 2,
        scratch_shapes=[
            vm((2, PAD, BS), BF16), vm((8, 2 * BS), BF16), vm((PAD, K), F32), vm((K, PAD), BF16),
            vm((K, W), F32), vm((2, W, BS), F32), vm((W, W), F32),
            vm((2, 2, BS), F32), vm((2, NS, 2, W), F32), vm((2, W), F32), vm((NS, 2, W), F32),
            vm((2, W, W), F32), vm((2, 1, W), F32), vm((2, 1, W), F32), vm((2, 1, BS), F32),
            vm((2, 16, BS), BF16),
            vm((2, 8, BS), F32), vm((2, 8, BS), F32), vm((2, W, W), F32), vm((2, W, W), F32),
            vm((2, W, W), F32), vm((4, 8, BS), F32),
            vm((2, 2, HW, BS), BF16), vm((2, 2, HW, BS), BF16),
            vm((2, 2, NT, HW, W), BF16), vm((2, 2, NT, HW, W), BF16), vm((2, 2, 8, W), F32),
            vm((2, K, BS), BF16),
            vm((2, 2, NV, PR, W), BF16), vm((2, 2, NV, PR, W), BF16), vm((2, 2, NV, PR, W), BF16),
            vm((PR, W), F32),
            dma((5,)), dma,
            dma((NS,)), dma((NS,)), dma((NS,)), dma((NS,)), dma((NT,)), dma((NT,)),
            dma((2, 16)), dma((2, 16)), dma((2, 16)), dma((2, 16)),
            dma((2, 2, 2)), dma((2, 2, 2)), dma((2, 2, NT)), dma((2, 2, NT)), dma((2,)), dma((2,)),
            dma((2, 2, NT)), dma((2, 2, NT)), dma((2, 2, NT)), dma((2, 2, NT)),
            dma((2, 2, NV)), dma((2, 2, NV)), dma((2, 2, NV)), dma((2, 2, NV)),
        ],
        compiler_params=pltpu.CompilerParams(
            collective_id=0, has_side_effects=True, vmem_limit_bytes=56 * 1024 * 1024),
    )(colors.T, genotypes, residual, coefficients, penalty.reshape(2, 1, BS))
    return (coef, res)


def solution(mesh):
    placed = (P("samp", "var"), P("samp", None), P("samp", "var"), P("var"), P(None, "var"))
    return jax.shard_map(
        shards,
        mesh=mesh,
        in_specs=placed,
        out_specs=(P("samp", "var"), P("samp", None)),
        check_vma=False,
    )
```

```python
import jax
import jax.numpy as jnp
from jax import lax
from jax.experimental import pallas as pl
from jax.experimental.pallas import tpu as pltpu
from jax.sharding import PartitionSpec as P

K = 256
BS = 2048
ROUNDS = 2
SAMPLES = 34560
ROWS = 1080
PAD = 1152
NS = 32
NT = 16
NV = 8
W = 128
HW = 64
YR = 272
PR = 136
MESH = pl.DeviceIdType.MESH
F32 = jnp.float32
BF16 = jnp.bfloat16
NN_T = (((1,), (1,)), ((), ()))


def al(x, m):
    return pl.multiple_of(x, m)


def zigzag(a, middle):
    return middle + (1 - 2 * (a % 2)) * ((a + 1) // 2)


def split(x):
    high = x.astype(BF16).astype(F32)
    return high, x - high


def kernel(
    colors, x_hbm, res_hbm, coef, pen,
    coef_out, res_out,
    xs, tail, rf, rt, rsum, g, gacc, st_loc, st_in, rg_loc, rg_in, fix, mean_own, scale_own, means, mhl,
    cb, stage, oldr, pick, newb, newt,
    pair_tx, pair_rx, rs_tx, rs_rx, nrm, dmat, c_tx, c_rx, t_buf,
    x_sem, t_sem, r_sem,
    st_ss, st_rs, rg_ss, rg_rs, mn_ss, mn_rs, old_ss, old_rs, new_ss, new_rs,
    pr_ss, pr_rs, rs_ss, rs_rs, nm_ss, nm_rs, ag_ss, ag_rs, fw_ss, fw_rs,
    cr_ss, cr_rs, ca_ss, ca_rs,
):
    s = lax.axis_index("samp")
    v = lax.axis_index("var")
    t = s // 2
    c = s % 2
    z = s // 4
    xh = t % 2
    yv = v % 4
    xv = v // 4
    partner = s + 1 - 2 * c
    holder = (s // 8) % 2
    place = pl.ds(al((s // 16) * HW + (s % 8) * 8, 8), 8)
    own_lanes = pl.ds(al(t * W, W), W)

    def chip(i):
        return ((z + zigzag(i // 2, 4)) % 8) * 2 + (xh + 1 - i % 2) % 2

    def group(i):
        return ((xv + 1 - i % 2) % 2) * 4 + (yv + zigzag(i // 2, 2)) % 4

    def rcopy(src, dst, ss, rs, samp, var):
        return pltpu.make_async_remote_copy(
            src_ref=src, dst_ref=dst, send_sem=ss, recv_sem=rs,
            device_id=(samp, var), device_id_type=MESH,
        )

    def arrived(ref, sem):
        rcopy(ref, ref, sem, sem, partner, v).wait_recv()

    def departed(ref, sem):
        rcopy(ref, ref, sem, sem, partner, v).wait_send()

    def chunk(a):
        return pl.ds(al(((z + zigzag(a, 4)) % 8) * 256, 256), 256)

    def x_copy(b, a):
        return pltpu.make_async_copy(
            x_hbm.at[pl.ds(0, 1072), pl.ds(al(b * BS + ((z + zigzag(a, 4)) % 8) * 256, 256), 256)],
            xs.at[b, pl.ds(0, 1072), chunk(a)], x_sem.at[b, a])

    tcopy = pltpu.make_async_copy(x_hbm.at[pl.ds(1072, 8), :], tail, t_sem)
    rcopy_in = pltpu.make_async_copy(res_hbm, rf.at[pl.ds(0, ROWS), :], r_sem)
    rcopy_in.start()
    tcopy.start()

    @pl.loop(0, 8)
    def _(a):
        for b in range(2):
            x_copy(b, a).start()

    barrier = pltpu.get_barrier_semaphore()

    @pl.loop(1, NS)
    def _(i):
        pl.semaphore_signal(barrier, inc=1, device_id=((s + i) % NS, v), device_id_type=MESH)

    @pl.loop(1, NV)
    def _(i):
        pl.semaphore_signal(barrier, inc=1, device_id=(s, (v + i) % NV), device_id_type=MESH)

    for b in range(2):
        cb[b] = coef[:, pl.ds(b * BS, BS)]
        newt[2 + b] = coef[:, pl.ds(b * BS, BS)]
    for r in range(ROUNDS):
        stage[r] = cb[colors[0, r]]

    def transposed(h):
        for i in range(PAD // W):
            rt[h, pl.ds(0, W), pl.ds(i * W, W)] = rf[pl.ds(i * W, W), pl.ds(h * W, W)].T.astype(BF16)
        rsum[pl.ds(h * W, W), :] = jnp.broadcast_to(
            jnp.sum(rt[h, pl.ds(0, W), :].astype(F32), axis=1, keepdims=True), (W, W))

    rf[pl.ds(ROWS, PAD - ROWS), :] = jnp.zeros((PAD - ROWS, K), F32)
    for h in range(2):
        rt[h, pl.ds(W, 16), :] = jnp.ones((16, PAD), BF16)
    for r in range(ROUNDS):
        for h in range(2):
            rs_rx[r, h, t] = jnp.zeros((HW, W), BF16)
            c_rx[r, h, v] = jnp.zeros((PR, W), BF16)
    rcopy_in.wait()
    transposed(0)
    transposed(1)
    for h in range(2):
        rg_loc[pl.ds(h, 1), :] = jnp.sum(
            rf[:, pl.ds(h * W, W)].astype(BF16).astype(F32), axis=0, keepdims=True)
    tcopy.wait()
    for b in range(2):
        xs[b, pl.ds(1088, PAD - 1088), :] = jnp.zeros((PAD - 1088, BS), BF16)
        xs[b, pl.ds(1072, 16), :] = jnp.concatenate(
            [tail[:, pl.ds(b * BS, BS)].astype(F32), jnp.zeros((8, BS), F32)], axis=0).astype(BF16)

    def st_copy(p):
        return rcopy(st_loc.at[:, :, pl.ds(al(p // 2 * W, W), W)], st_in.at[:, s], st_ss, st_rs, p, v)

    def rg_copy(p):
        return rcopy(rg_loc, rg_in.at[s], rg_ss, rg_rs, p, v)

    def old_copy(r, j):
        return rcopy(stage.at[r, :, pl.ds(al(j * W, W), W)], oldr.at[r, place, :],
                     old_ss.at[r], old_rs.at[r], 2 * j + holder, v)

    def old_sends(r):
        @pl.loop(0, NT)
        def _(j):
            @pl.when(2 * j + holder != s)
            def _():
                old_copy(r, j).start()

            @pl.when(2 * j + holder == s)
            def _():
                oldr[r, place, :] = stage[r, :, pl.ds(al(j * W, W), W)]

    def each(wait, some, every):
        @pl.when(holder == c)
        def _():
            wait(some)

        @pl.when(holder != c)
        def _():
            wait(every)

    def old_drain(r):
        each(lambda ref: departed(ref, old_ss.at[r]), oldr.at[r, pl.ds(0, W - 8), :], oldr.at[r])

    def sharer(i):
        return (i // 8) * 16 + c * 8 + i % 8

    def old_wait(r):
        each(lambda ref: arrived(ref, old_rs.at[r]), oldr.at[r, pl.ds(0, W - 8), :], oldr.at[r])

    def new_copy(r, i):
        return rcopy(newb.at[r, pl.ds(al(i * 8, 8), 8), :], newt.at[r, :, own_lanes],
                     new_ss.at[r], new_rs.at[r], sharer(i), v)

    def new_wait(r):
        each(lambda ref: arrived(ref, new_rs.at[r]), newt.at[r, :, pl.ds(0, BS - W)], newt.at[r])

    def new_drain(r):
        each(lambda ref: departed(ref, new_ss.at[r]), newb.at[r, pl.ds(0, W - 8), :], newb.at[r])

    def ca_copy(r, h, p):
        return rcopy(t_buf.at[r, h, v], t_buf.at[r, h, v], ca_ss.at[r, h], ca_rs.at[r, h], s, p)

    def ca_drain(r, h):
        departed(t_buf.at[r, h, pl.ds(0, NV - 1)], ca_ss.at[r, h])

    def own_rows(h):
        return pl.ds(al(c * HW, HW), HW)

    def pair_copy(r, h, a):
        return rcopy(pair_tx.at[r, h, :, chunk(a)], pair_rx.at[r, h, :, chunk(a)],
                     pr_ss.at[r, h], pr_rs.at[r, h, a], partner, v)

    def moments(a):
        lanes = chunk(a)

        @pl.loop(0, 2)
        def _(b):
            cnt = jnp.zeros((16, 256), F32)
            sqr = jnp.zeros((16, 256), F32)
            for e in range(2):
                x = xs[b, pl.ds(e * 576, 16), lanes]
                one = x
                two = x * x
                for i in range(1, 36):
                    x = xs[b, pl.ds(e * 576 + i * 16, 16), lanes]
                    one = one + x
                    two = two + x * x
                cnt = cnt + one.astype(F32)
                sqr = sqr + two.astype(F32)
            st_loc[b, pl.ds(0, 1), lanes] = jnp.sum(cnt, axis=0, keepdims=True)
            st_loc[b, pl.ds(1, 1), lanes] = jnp.sum(sqr, axis=0, keepdims=True)

    def product(r, h, a, send=True):
        lanes = chunk(a)
        if r == 0:
            out = jnp.dot(rt[h], xs[colors[0, r], :, lanes], preferred_element_type=F32)
            mean = out[W:W + 1] * (1.0 / ROWS)
            out = out[:W]
        else:
            out = jnp.dot(rt[h, pl.ds(0, W), :], xs[colors[0, r], :, lanes], preferred_element_type=F32)
            mean = means[colors[0, r], :, lanes]
        g[h, :, lanes] = out - rsum[pl.ds(h * W, W), :][:, 0:1] * mean
        pair_tx[r, h, :, lanes] = g[h, pl.ds(al((1 - c) * HW, HW), HW), lanes].astype(BF16)
        if send:
            pair_copy(r, h, a).start()

    def rs_copy(r, h, j):
        return rcopy(rs_tx.at[r, h, j], rs_rx.at[r, h, t], rs_ss.at[r, h], rs_rs.at[r, h], 2 * j + c, v)

    def send_on(r, h, a):
        lanes = chunk(a)
        pair_copy(r, h, a).wait_recv()
        mine = g[h, own_rows(h), lanes] + pair_rx[r, h, :, lanes].astype(F32)
        g[h, own_rows(h), lanes] = mine
        low = mine.astype(BF16)
        for e in range(2):
            j = ((z + zigzag(a, 4)) % 8) * 2 + e
            rs_tx[r, h, j] = low[:, e * W:(e + 1) * W]

            @pl.when(j != t)
            def _():
                rs_copy(r, h, j).start()

    def gradient(r, h):
        @pl.loop(0, 4)
        def _(a):
            product(r, h, a, send=r + h > 0)

        if r + h == 0:
            pl.semaphore_wait(barrier, NS - 1 + NV - 1)

            @pl.loop(0, 4)
            def _(a):
                pair_copy(0, 0, a).start()

            @pl.loop(1, NS)
            def _(i):
                rg_copy((s + i) % NS).start()

            rg_in[s] = rg_loc[...]
            old_sends(0)

        @pl.loop(4, 8)
        def _(a):
            product(r, h, a)
            send_on(r, h, a - 4)

        @pl.loop(4, 8)
        def _(a):
            send_on(r, h, a)

    @pl.loop(0, 8)
    def _(a):
        for b in range(2):
            x_copy(b, a).wait()
        moments(a)

    gradient(0, 0)

    @pl.loop(1, NS)
    def _(i):
        st_copy((s + i) % NS).start()

    st_in[:, s] = st_loc[:, :, own_lanes]
    gradient(0, 1)

    def mn_copy(j):
        return rcopy(mean_own, means.at[:, :, own_lanes], mn_ss, mn_rs, 2 * j + c, v)

    st_all = st_in.at[:, pl.ds(0, NS - 1)]
    rg_all = rg_in.at[pl.ds(0, NS - 1)]
    mn_all = means.at[:, :, pl.ds(0, (NT - 1) * W)]

    def statistics():
        arrived(st_all, st_rs)
        arrived(rg_all, rg_rs)

        for b in range(2):
            total = jnp.sum(st_in[b], axis=0)
            mean = total[0:1] / SAMPLES
            mean_own[b] = mean
            means[b, :, own_lanes] = mean
            scale_own[b] = total[1:2] - total[0:1] * mean

        @pl.loop(0, NT - 1)
        def _(i):
            mn_copy(chip(i)).start()

        b_high, b_low = split(st_in[colors[0, 0]][:, 0, :] * (1.0 / ROWS) - mean_own[colors[0, 0]])
        right = jnp.concatenate([b_high, b_low, b_high, b_low], axis=0).astype(BF16)
        for h in range(2):
            a_high, a_low = split(rg_in[:, h, :])
            left = jnp.concatenate([a_high, a_high, a_low, a_low], axis=0)
            fix[h] = jnp.dot(left.T.astype(BF16), right, preferred_element_type=F32)
            gacc[pl.ds(h * HW, HW), :] = gacc[pl.ds(h * HW, HW), :] + fix[h, own_rows(h), :]

    def d_view(r, h, core, j):
        return dmat.at[r, pl.ds(al(h * W + core * HW, HW), HW), pl.ds(al(j * W, W), W)]

    def ag_copy(r, h, j, i_src):
        return rcopy(d_view(r, h, c, i_src), d_view(r, h, c, i_src), ag_ss.at[r, h], ag_rs.at[r, h, i_src],
                     2 * j + c, v)

    def fw_copy(r, h, j):
        return rcopy(d_view(r, h, c, j), d_view(r, h, c, j), fw_ss.at[r, h], fw_rs.at[r, h], partner, v)

    def cr_copy(r, h, p):
        return rcopy(c_tx.at[r, h, p], c_rx.at[r, h, v], cr_ss.at[r, h], cr_rs.at[r, h], s, p)

    def ag_drain(r):
        for h in range(2):
            departed(dmat.at[r, pl.ds(0, HW), pl.ds(0, (NT - 1) * W)], ag_ss.at[r, h])
            departed(dmat.at[r, pl.ds(0, HW), :], fw_ss.at[r, h])

    def cr_drain(r):
        for h in range(2):
            departed(c_tx.at[r, h, pl.ds(0, NV - 1)], cr_ss.at[r, h])

    for r in range(ROUNDS):
        color = colors[0, r]

        if r == 1:
            ag_drain(0)
            cr_drain(0)

        for h in range(2):
            rows = pl.ds(h * HW, HW)
            arrived(rs_rx.at[r, h, pl.ds(0, NT - 1)], rs_rs.at[r, h])
            total = g[h, own_rows(h), own_lanes]
            for j in range(NT):
                total = total + rs_rx[r, h, j].astype(F32)
            gacc[rows, :] = total

        old_wait(r)
        if r == 0:
            statistics()
            old = oldr[0]
        else:
            pick[0] = oldr[1]
            gap = color - colors[0, 0]
            old = pick[1 - gap * gap]
        scale = scale_own[color]
        shifted = old + gacc[...] / scale
        part = jnp.sum(shifted * shifted, axis=0, keepdims=True)
        nrm[r, 0] = jnp.broadcast_to(part, (8, W))
        ncopy = rcopy(nrm.at[r, 0], nrm.at[r, 1], nm_ss.at[r], nm_rs.at[r], partner, v)
        ncopy.start()
        push = pen[color, :, own_lanes] * jnp.sqrt(K / scale)
        ncopy.wait_recv()
        norm = jnp.sqrt(part + nrm[r, 1][0:1] + 1e-06)
        new = jnp.maximum(0.0, 1.0 - push / norm) * shifted
        change = (new - old).astype(BF16)
        for h in range(2):
            dmat[r, pl.ds(al(h * W + c * HW, HW), HW), own_lanes] = change[h * HW:(h + 1) * HW]
        newb[r] = new
        if r == 0:
            pick[1] = new

        for h in range(2):
            @pl.loop(0, NT - 1)
            def _(i):
                ag_copy(r, h, chip(i), t).start()

            fw_copy(r, h, t).start()

        if r == 0:
            departed(st_all, st_ss)
            departed(rg_all, rg_ss)
            departed(mn_all, mn_ss)
            old_drain(0)
            arrived(mn_all, mn_rs)
            for b in range(2):
                high, low = split(means[b])
                mhl[b] = jnp.concatenate(
                    [jnp.broadcast_to(high, (8, BS)), jnp.broadcast_to(low, (8, BS))], axis=0).astype(BF16)
        else:
            old_drain(1)
            new_drain(0)
            ca_drain(0, 0)
            ca_drain(0, 1)
        ncopy.wait_send()
        for h in range(2):
            departed(pair_tx.at[r, h], pr_ss.at[r, h])
            departed(rs_tx.at[r, h, pl.ds(0, NT - 1)], rs_ss.at[r, h])

        for h in range(2):
            @pl.loop(0, NT - 1)
            def _(i):
                j = chip(i)
                ag_copy(r, h, j, j).wait_recv()
                fw_copy(r, h, j).start()

            arrived(dmat.at[r, pl.ds(0, HW), :], fw_rs.at[r, h])

            rows = pl.ds(h * W, W)
            md = lax.dot_general(mhl[color], dmat[r, rows, :], NN_T, preferred_element_type=F32)
            md = md[0:1] + md[8:9]

            @pl.loop(0, 4)
            def _(i):
                y = (yv + zigzag(i, 2)) % 4
                out = lax.dot_general(xs[color, pl.ds(al(y * YR, 16), YR), :], dmat[r, rows, :], NN_T,
                                      preferred_element_type=F32) - md
                for w in range(2):
                    c_tx[r, h, w * 4 + y] = out[w * PR:(w + 1) * PR].astype(BF16)
                for w in range(2):
                    p = w * 4 + y

                    @pl.when(p != v)
                    def _():
                        cr_copy(r, h, p).start()

        def add_up(h):
            arrived(c_rx.at[r, h, pl.ds(0, NV - 1)], cr_rs.at[r, h])
            total = c_tx[r, h, v].astype(F32)
            for p in range(NV):
                total = total + c_rx[r, h, p].astype(F32)
            t_buf[r, h, v] = total.astype(BF16)

            @pl.loop(0, NV - 1)
            def _(i):
                ca_copy(r, h, group(i)).start()

        add_up(0)

        @pl.loop(0, 16)
        def _(i):
            @pl.when(sharer(i) != s)
            def _():
                new_copy(r, i).start()

            @pl.when(sharer(i) == s)
            def _():
                newt[r, :, own_lanes] = newb[r, pl.ds(al(i * 8, 8), 8), :]

        if r == 0:
            old_sends(1)
        else:
            ag_drain(1)

        add_up(1)

        if r == 1:
            cr_drain(r)

        if r == 1:
            new_wait(0)
            new_wait(1)

            for b in range(2):
                d0 = colors[0, 0] - b
                d1 = colors[0, 1] - b
                coef_out[:, pl.ds(b * BS, BS)] = newt[1 - d1 * d1 + d1 * d1 * d0 * d0 * (2 + b)]
            new_drain(r)

        for h in range(2):
            lanes = pl.ds(h * W, W)

            arrived(t_buf.at[r, h, pl.ds(0, NV - 1)], ca_rs.at[r, h])
            for p in range(NV):
                rows = pl.ds((p % 4) * YR + (p // 4) * PR, PR)
                rf[rows, lanes] = rf[rows, lanes] - t_buf[r, h, p].astype(F32)

            if r == 0:
                rf[pl.ds(ROWS, 8), lanes] = jnp.zeros((8, W), F32)
                transposed(h)
                gradient(1, h)
            else:
                res_out[:, lanes] = rf[pl.ds(0, ROWS), lanes]

    ca_drain(1, 0)
    ca_drain(1, 1)


def shards(genotypes, residual, coefficients, penalty, colors):
    dma = pltpu.SemaphoreType.DMA
    vm = pltpu.VMEM
    coef, res = pl.pallas_call(
        kernel,
        out_shape=(jax.ShapeDtypeStruct((8, 2 * BS), F32), jax.ShapeDtypeStruct((ROWS, K), F32)),
        in_specs=[
            pl.BlockSpec(memory_space=pltpu.SMEM),
            pl.BlockSpec(memory_space=pl.ANY),
            pl.BlockSpec(memory_space=pl.ANY),
            pl.BlockSpec(memory_space=pltpu.VMEM),
            pl.BlockSpec(memory_space=pltpu.VMEM),
        ],
        out_specs=[pl.BlockSpec(memory_space=pltpu.VMEM)] * 2,
        scratch_shapes=[
            vm((2, PAD, BS), BF16), vm((8, 2 * BS), BF16), vm((PAD, K), F32), vm((2, W + 16, PAD), BF16),
            vm((K, W), F32), vm((2, W, BS), F32), vm((W, W), F32),
            vm((2, 2, BS), F32), vm((2, NS, 2, W), F32), vm((2, W), F32), vm((NS, 2, W), F32),
            vm((2, W, W), F32), vm((2, 1, W), F32), vm((2, 1, W), F32), vm((2, 1, BS), F32),
            vm((2, 16, BS), BF16),
            vm((2, 8, BS), F32), vm((2, 8, BS), F32), vm((2, W, W), F32), vm((2, W, W), F32),
            vm((2, W, W), F32), vm((4, 8, BS), F32),
            vm((2, 2, HW, BS), BF16), vm((2, 2, HW, BS), BF16),
            vm((2, 2, NT, HW, W), BF16), vm((2, 2, NT, HW, W), BF16), vm((2, 2, 8, W), F32),
            vm((2, K, BS), BF16),
            vm((2, 2, NV, PR, W), BF16), vm((2, 2, NV, PR, W), BF16), vm((2, 2, NV, PR, W), BF16),
            dma((2, 8)), dma, dma,
            dma, dma, dma, dma, dma, dma, dma((2,)), dma((2,)), dma((2,)), dma((2,)),
            dma((2, 2)), dma((2, 2, 8)), dma((2, 2)), dma((2, 2)), dma((2,)), dma((2,)),
            dma((2, 2)), dma((2, 2, NT)), dma((2, 2)), dma((2, 2)),
            dma((2, 2)), dma((2, 2)), dma((2, 2)), dma((2, 2)),
        ],
        compiler_params=pltpu.CompilerParams(
            collective_id=0, has_side_effects=True, vmem_limit_bytes=56 * 1024 * 1024),
    )(colors.T, genotypes, residual, coefficients, penalty.reshape(2, 1, BS))
    return (coef, res)


def solution(mesh):
    placed = (P("samp", "var"), P("samp", None), P("samp", "var"), P("var"), P(None, "var"))
    return jax.shard_map(
        shards,
        mesh=mesh,
        in_specs=placed,
        out_specs=(P("samp", "var"), P("samp", None)),
        check_vma=False,
    )
```

```python
import jax
import jax.numpy as jnp
from jax import lax
from jax.experimental import pallas as pl
from jax.experimental.pallas import tpu as pltpu
from jax.sharding import PartitionSpec as P

K = 256
BS = 2048
ROUNDS = 2
SAMPLES = 34560
ROWS = 1080
PAD = 1152
NS = 32
NT = 16
NV = 8
W = 128
HW = 64
YR = 272
PR = 136
MESH = pl.DeviceIdType.MESH
F32 = jnp.float32
BF16 = jnp.bfloat16
NN_T = (((1,), (1,)), ((), ()))


def al(x, m):
    return pl.multiple_of(x, m)


def zigzag(a, middle):
    return middle + (1 - 2 * (a % 2)) * ((a + 1) // 2)


def split(x):
    high = x.astype(BF16).astype(F32)
    return high, x - high


def kernel(
    colors, x_hbm, res_hbm, coef, pen,
    coef_out, res_out,
    xs, tail, rf, rt, rsum, g, gacc, st_loc, st_in, rg_loc, rg_in, fix, mean_own, scale_own, means, mhl,
    cb, stage, oldr, pick, newb, newt,
    pair_tx, pair_rx, rs_tx, rs_rx, nrm, dmat, c_tx, c_rx, t_buf, cout,
    x_sem, t_sem, r_sem, o_sem,
    st_ss, st_rs, rg_ss, rg_rs, mn_ss, mn_rs, old_ss, old_rs, new_ss, new_rs,
    pr_ss, pr_rs, rs_ss, rs_rs, nm_ss, nm_rs, ag_ss, ag_rs, fw_ss, fw_rs,
    cr_ss, cr_rs, ca_ss, ca_rs,
):
    s = lax.axis_index("samp")
    v = lax.axis_index("var")
    t = s // 2
    c = s % 2
    z = s // 4
    xh = t % 2
    yv = v % 4
    xv = v // 4
    partner = s + 1 - 2 * c
    holder = (s // 8) % 2
    place = pl.ds(al((s // 16) * HW + (s % 8) * 8, 8), 8)
    own_lanes = pl.ds(al(t * W, W), W)

    def chip(i):
        return ((z + zigzag(i // 2, 4)) % 8) * 2 + (xh + 1 - i % 2) % 2

    def group(i):
        return ((xv + 1 - i % 2) % 2) * 4 + (yv + zigzag(i // 2, 2)) % 4

    def rcopy(src, dst, ss, rs, samp, var):
        return pltpu.make_async_remote_copy(
            src_ref=src, dst_ref=dst, send_sem=ss, recv_sem=rs,
            device_id=(samp, var), device_id_type=MESH,
        )

    def arrived(ref, sem):
        rcopy(ref, ref, sem, sem, partner, v).wait_recv()

    def departed(ref, sem):
        rcopy(ref, ref, sem, sem, partner, v).wait_send()

    def chunk(a):
        return pl.ds(al(((z + zigzag(a, 4)) % 8) * 256, 256), 256)

    def x_copy(b, a):
        return pltpu.make_async_copy(
            x_hbm.at[pl.ds(0, 1072), pl.ds(al(b * BS + ((z + zigzag(a, 4)) % 8) * 256, 256), 256)],
            xs.at[b, pl.ds(0, 1072), chunk(a)], x_sem.at[b, a])

    tcopy = pltpu.make_async_copy(x_hbm.at[pl.ds(1072, 8), :], tail, t_sem)
    rcopy_in = pltpu.make_async_copy(res_hbm, rf.at[pl.ds(0, ROWS), :], r_sem)
    rcopy_in.start()
    tcopy.start()

    @pl.loop(0, 8)
    def _(a):
        for b in range(2):
            x_copy(b, a).start()

    coef_copy = pltpu.make_async_copy(cout, coef_out, o_sem.at[2])

    def res_copy(h):
        lanes = pl.ds(h * W, W)
        return pltpu.make_async_copy(rf.at[pl.ds(0, ROWS), lanes], res_out.at[:, lanes], o_sem.at[h])

    barrier = pltpu.get_barrier_semaphore()

    @pl.loop(1, NS)
    def _(i):
        pl.semaphore_signal(barrier, inc=1, device_id=((s + i) % NS, v), device_id_type=MESH)

    @pl.loop(1, NV)
    def _(i):
        pl.semaphore_signal(barrier, inc=1, device_id=(s, (v + i) % NV), device_id_type=MESH)

    for b in range(2):
        cb[b] = coef[:, pl.ds(b * BS, BS)]
        newt[2 + b] = coef[:, pl.ds(b * BS, BS)]
    for r in range(ROUNDS):
        stage[r] = cb[colors[0, r]]

    def transposed(h):
        for i in range(PAD // W):
            rt[h, pl.ds(0, W), pl.ds(i * W, W)] = rf[pl.ds(i * W, W), pl.ds(h * W, W)].T.astype(BF16)
        rsum[pl.ds(h * W, W), :] = jnp.broadcast_to(
            jnp.sum(rt[h, pl.ds(0, W), :].astype(F32), axis=1, keepdims=True), (W, W))

    rf[pl.ds(ROWS, PAD - ROWS), :] = jnp.zeros((PAD - ROWS, K), F32)
    for h in range(2):
        rt[h, pl.ds(W, 16), :] = jnp.ones((16, PAD), BF16)
    for r in range(ROUNDS):
        for h in range(2):
            rs_rx[r, h, t] = jnp.zeros((HW, W), BF16)
            c_rx[r, h, v] = jnp.zeros((PR, W), BF16)
    rcopy_in.wait()
    transposed(0)
    transposed(1)
    for h in range(2):
        rg_loc[pl.ds(h, 1), :] = jnp.sum(
            rf[:, pl.ds(h * W, W)].astype(BF16).astype(F32), axis=0, keepdims=True)
    tcopy.wait()
    for b in range(2):
        xs[b, pl.ds(1088, PAD - 1088), :] = jnp.zeros((PAD - 1088, BS), BF16)
        xs[b, pl.ds(1072, 16), :] = jnp.concatenate(
            [tail[:, pl.ds(b * BS, BS)].astype(F32), jnp.zeros((8, BS), F32)], axis=0).astype(BF16)

    def st_copy(p):
        return rcopy(st_loc.at[:, :, pl.ds(al(p // 2 * W, W), W)], st_in.at[:, s], st_ss, st_rs, p, v)

    def rg_copy(p):
        return rcopy(rg_loc, rg_in.at[s], rg_ss, rg_rs, p, v)

    def old_copy(r, j):
        return rcopy(stage.at[r, :, pl.ds(al(j * W, W), W)], oldr.at[r, place, :],
                     old_ss.at[r], old_rs.at[r], 2 * j + holder, v)

    def old_sends(r):
        @pl.loop(0, NT)
        def _(j):
            @pl.when(2 * j + holder != s)
            def _():
                old_copy(r, j).start()

            @pl.when(2 * j + holder == s)
            def _():
                oldr[r, place, :] = stage[r, :, pl.ds(al(j * W, W), W)]

    def each(wait, some, every):
        @pl.when(holder == c)
        def _():
            wait(some)

        @pl.when(holder != c)
        def _():
            wait(every)

    def old_drain(r):
        each(lambda ref: departed(ref, old_ss.at[r]), oldr.at[r, pl.ds(0, W - 8), :], oldr.at[r])

    def sharer(i):
        return (i // 8) * 16 + c * 8 + i % 8

    def old_wait(r):
        each(lambda ref: arrived(ref, old_rs.at[r]), oldr.at[r, pl.ds(0, W - 8), :], oldr.at[r])

    def new_copy(r, i):
        return rcopy(newb.at[r, pl.ds(al(i * 8, 8), 8), :], newt.at[r, :, own_lanes],
                     new_ss.at[r], new_rs.at[r], sharer(i), v)

    def new_wait(r):
        each(lambda ref: arrived(ref, new_rs.at[r]), newt.at[r, :, pl.ds(0, BS - W)], newt.at[r])

    def new_drain(r):
        each(lambda ref: departed(ref, new_ss.at[r]), newb.at[r, pl.ds(0, W - 8), :], newb.at[r])

    def ca_copy(r, h, p):
        return rcopy(t_buf.at[r, h, v], t_buf.at[r, h, v], ca_ss.at[r, h], ca_rs.at[r, h], s, p)

    def ca_drain(r, h):
        departed(t_buf.at[r, h, pl.ds(0, NV - 1)], ca_ss.at[r, h])

    def own_rows(h):
        return pl.ds(al(c * HW, HW), HW)

    def pair_copy(r, h, a):
        return rcopy(pair_tx.at[r, h, :, chunk(a)], pair_rx.at[r, h, :, chunk(a)],
                     pr_ss.at[r, h], pr_rs.at[r, h, a], partner, v)

    def moments(a):
        lanes = chunk(a)

        @pl.loop(0, 2)
        def _(b):
            cnt = jnp.zeros((16, 256), F32)
            sqr = jnp.zeros((16, 256), F32)
            for e in range(2):
                x = xs[b, pl.ds(e * 576, 16), lanes]
                one = x
                two = x * x
                for i in range(1, 36):
                    x = xs[b, pl.ds(e * 576 + i * 16, 16), lanes]
                    one = one + x
                    two = two + x * x
                cnt = cnt + one.astype(F32)
                sqr = sqr + two.astype(F32)
            st_loc[b, pl.ds(0, 1), lanes] = jnp.sum(cnt, axis=0, keepdims=True)
            st_loc[b, pl.ds(1, 1), lanes] = jnp.sum(sqr, axis=0, keepdims=True)

    def product(r, h, a, send=True):
        lanes = chunk(a)
        if r == 0:
            out = jnp.dot(rt[h], xs[colors[0, r], :, lanes], preferred_element_type=F32)
            mean = out[W:W + 1] * (1.0 / ROWS)
            out = out[:W]
        else:
            out = jnp.dot(rt[h, pl.ds(0, W), :], xs[colors[0, r], :, lanes], preferred_element_type=F32)
            mean = means[colors[0, r], :, lanes]
        g[h, :, lanes] = out - rsum[pl.ds(h * W, W), :][:, 0:1] * mean
        pair_tx[r, h, :, lanes] = g[h, pl.ds(al((1 - c) * HW, HW), HW), lanes].astype(BF16)
        if send:
            pair_copy(r, h, a).start()

    def rs_copy(r, h, j):
        return rcopy(rs_tx.at[r, h, j], rs_rx.at[r, h, t], rs_ss.at[r, h], rs_rs.at[r, h], 2 * j + c, v)

    def send_on(r, h, a):
        lanes = chunk(a)
        pair_copy(r, h, a).wait_recv()
        mine = g[h, own_rows(h), lanes] + pair_rx[r, h, :, lanes].astype(F32)
        g[h, own_rows(h), lanes] = mine
        low = mine.astype(BF16)
        for e in range(2):
            j = ((z + zigzag(a, 4)) % 8) * 2 + e
            rs_tx[r, h, j] = low[:, e * W:(e + 1) * W]

            @pl.when(j != t)
            def _():
                rs_copy(r, h, j).start()

    def gradient(r, h):
        @pl.loop(0, 4)
        def _(a):
            product(r, h, a, send=r + h > 0)

        if r + h == 0:
            pl.semaphore_wait(barrier, NS - 1 + NV - 1)

            @pl.loop(0, 4)
            def _(a):
                pair_copy(0, 0, a).start()

            @pl.loop(1, NS)
            def _(i):
                rg_copy((s + i) % NS).start()

            rg_in[s] = rg_loc[...]
            old_sends(0)

        @pl.loop(4, 8)
        def _(a):
            product(r, h, a)
            send_on(r, h, a - 4)

        @pl.loop(4, 8)
        def _(a):
            send_on(r, h, a)

    @pl.loop(0, 8)
    def _(a):
        for b in range(2):
            x_copy(b, a).wait()
        moments(a)

    gradient(0, 0)

    @pl.loop(1, NS)
    def _(i):
        st_copy((s + i) % NS).start()

    st_in[:, s] = st_loc[:, :, own_lanes]
    gradient(0, 1)

    def mn_copy(j):
        return rcopy(mean_own, means.at[:, :, own_lanes], mn_ss, mn_rs, 2 * j + c, v)

    st_all = st_in.at[:, pl.ds(0, NS - 1)]
    rg_all = rg_in.at[pl.ds(0, NS - 1)]
    mn_all = means.at[:, :, pl.ds(0, (NT - 1) * W)]

    def statistics():
        arrived(st_all, st_rs)
        arrived(rg_all, rg_rs)

        for b in range(2):
            total = jnp.sum(st_in[b], axis=0)
            mean = total[0:1] / SAMPLES
            mean_own[b] = mean
            means[b, :, own_lanes] = mean
            scale_own[b] = total[1:2] - total[0:1] * mean

        @pl.loop(0, NT - 1)
        def _(i):
            mn_copy(chip(i)).start()

        b_high, b_low = split(st_in[colors[0, 0]][:, 0, :] * (1.0 / ROWS) - mean_own[colors[0, 0]])
        right = jnp.concatenate([b_high, b_low, b_high, b_low], axis=0).astype(BF16)
        for h in range(2):
            a_high, a_low = split(rg_in[:, h, :])
            left = jnp.concatenate([a_high, a_high, a_low, a_low], axis=0)
            fix[h] = jnp.dot(left.T.astype(BF16), right, preferred_element_type=F32)
            gacc[pl.ds(h * HW, HW), :] = gacc[pl.ds(h * HW, HW), :] + fix[h, own_rows(h), :]

    def d_view(r, h, core, j):
        return dmat.at[r, pl.ds(al(h * W + core * HW, HW), HW), pl.ds(al(j * W, W), W)]

    def ag_copy(r, h, j):
        own = d_view(r, h, c, t)
        return rcopy(own, own, ag_ss.at[r, h], ag_rs.at[r, h, z], 2 * j + c, v)

    def level(r, h, k):
        return dmat.at[r, pl.ds(al(h * W + c * HW, HW), HW), pl.ds(al(k * 256, 256), 256)]

    def fw_copy(r, h, k):
        return rcopy(level(r, h, k), level(r, h, k), fw_ss.at[r, h], fw_rs.at[r, h], partner, v)

    def cr_copy(r, h, p):
        return rcopy(c_tx.at[r, h, p], c_rx.at[r, h, v], cr_ss.at[r, h], cr_rs.at[r, h], s, p)

    def ag_drain(r):
        for h in range(2):
            departed(dmat.at[r, pl.ds(0, HW), pl.ds(0, (NT - 1) * W)], ag_ss.at[r, h])
            departed(dmat.at[r, pl.ds(0, HW), :], fw_ss.at[r, h])

    def cr_drain(r):
        for h in range(2):
            departed(c_tx.at[r, h, pl.ds(0, NV - 1)], cr_ss.at[r, h])

    for r in range(ROUNDS):
        color = colors[0, r]

        if r == 1:
            ag_drain(0)
            cr_drain(0)

        for h in range(2):
            rows = pl.ds(h * HW, HW)
            arrived(rs_rx.at[r, h, pl.ds(0, NT - 1)], rs_rs.at[r, h])
            total = g[h, own_rows(h), own_lanes]
            for j in range(NT):
                total = total + rs_rx[r, h, j].astype(F32)
            gacc[rows, :] = total

        old_wait(r)
        if r == 0:
            statistics()
            old = oldr[0]
        else:
            pick[0] = oldr[1]
            gap = color - colors[0, 0]
            old = pick[1 - gap * gap]
        scale = scale_own[color]
        shifted = old + gacc[...] / scale
        part = jnp.sum(shifted * shifted, axis=0, keepdims=True)
        nrm[r, 0] = jnp.broadcast_to(part, (8, W))
        ncopy = rcopy(nrm.at[r, 0], nrm.at[r, 1], nm_ss.at[r], nm_rs.at[r], partner, v)
        ncopy.start()
        push = pen[color, :, own_lanes] * jnp.sqrt(K / scale)
        ncopy.wait_recv()
        norm = jnp.sqrt(part + nrm[r, 1][0:1] + 1e-06)
        new = jnp.maximum(0.0, 1.0 - push / norm) * shifted
        change = (new - old).astype(BF16)
        for h in range(2):
            dmat[r, pl.ds(al(h * W + c * HW, HW), HW), own_lanes] = change[h * HW:(h + 1) * HW]
        newb[r] = new
        if r == 0:
            pick[1] = new

        for h in range(2):
            @pl.loop(0, NT - 1)
            def _(i):
                ag_copy(r, h, chip(i)).start()


        if r == 0:
            departed(st_all, st_ss)
            departed(rg_all, rg_ss)
            departed(mn_all, mn_ss)
            old_drain(0)
            arrived(mn_all, mn_rs)
            for b in range(2):
                high, low = split(means[b])
                mhl[b] = jnp.concatenate(
                    [jnp.broadcast_to(high, (8, BS)), jnp.broadcast_to(low, (8, BS))], axis=0).astype(BF16)
        else:
            old_drain(1)
            new_drain(0)
            ca_drain(0, 0)
            ca_drain(0, 1)
        ncopy.wait_send()
        for h in range(2):
            departed(pair_tx.at[r, h], pr_ss.at[r, h])
            departed(rs_tx.at[r, h, pl.ds(0, NT - 1)], rs_ss.at[r, h])

        for h in range(2):
            @pl.loop(0, 7)
            def _(a):
                k = (z + zigzag(a, 4)) % 8
                arrived(level(r, h, k), ag_rs.at[r, h, k])
                fw_copy(r, h, k).start()

            arrived(d_view(r, h, c, t + 1 - 2 * xh), ag_rs.at[r, h, z])
            fw_copy(r, h, z).start()

            arrived(dmat.at[r, pl.ds(0, HW), :], fw_rs.at[r, h])

            rows = pl.ds(h * W, W)
            md = lax.dot_general(mhl[color], dmat[r, rows, :], NN_T, preferred_element_type=F32)
            md = md[0:1] + md[8:9]

            @pl.loop(0, 4)
            def _(i):
                y = (yv + zigzag(i, 2)) % 4
                out = lax.dot_general(xs[color, pl.ds(al(y * YR, 16), YR), :], dmat[r, rows, :], NN_T,
                                      preferred_element_type=F32) - md
                for w in range(2):
                    c_tx[r, h, w * 4 + y] = out[w * PR:(w + 1) * PR].astype(BF16)
                for w in range(2):
                    p = w * 4 + y

                    @pl.when(p != v)
                    def _():
                        cr_copy(r, h, p).start()

        def add_up(h):
            arrived(c_rx.at[r, h, pl.ds(0, NV - 1)], cr_rs.at[r, h])
            total = c_tx[r, h, v].astype(F32)
            for p in range(NV):
                total = total + c_rx[r, h, p].astype(F32)
            t_buf[r, h, v] = total.astype(BF16)

            @pl.loop(0, NV - 1)
            def _(i):
                ca_copy(r, h, group(i)).start()

        add_up(0)

        @pl.loop(0, 16)
        def _(i):
            @pl.when(sharer(i) != s)
            def _():
                new_copy(r, i).start()

            @pl.when(sharer(i) == s)
            def _():
                newt[r, :, own_lanes] = newb[r, pl.ds(al(i * 8, 8), 8), :]

        if r == 0:
            old_sends(1)
        else:
            ag_drain(1)

        add_up(1)

        if r == 1:
            cr_drain(r)

        if r == 1:
            new_wait(0)
            new_wait(1)

            for b in range(2):
                d0 = colors[0, 0] - b
                d1 = colors[0, 1] - b
                cout[:, pl.ds(b * BS, BS)] = newt[1 - d1 * d1 + d1 * d1 * d0 * d0 * (2 + b)]
            coef_copy.start()
            new_drain(r)

        for h in range(2):
            lanes = pl.ds(h * W, W)

            arrived(t_buf.at[r, h, pl.ds(0, NV - 1)], ca_rs.at[r, h])
            for p in range(NV):
                rows = pl.ds((p % 4) * YR + (p // 4) * PR, PR)
                rf[rows, lanes] = rf[rows, lanes] - t_buf[r, h, p].astype(F32)

            if r == 0:
                rf[pl.ds(ROWS, 8), lanes] = jnp.zeros((8, W), F32)
                transposed(h)
                gradient(1, h)
            else:
                res_copy(h).start()

    ca_drain(1, 0)
    ca_drain(1, 1)
    coef_copy.wait()
    res_copy(0).wait()
    res_copy(1).wait()


def hand_over(coef, res, coef_out, res_out, coef_vmem, res_vmem, in_sems, out_sems):
    pieces = [(coef, coef_vmem, coef_out)]
    for q in range(3):
        rows = pl.ds(q * 360, 360)
        pieces.append((res.at[rows, :], res_vmem.at[rows, :], res_out.at[rows, :]))
    loads = [pltpu.make_async_copy(a, b, in_sems.at[q]) for q, (a, b, _) in enumerate(pieces)]
    stores = [pltpu.make_async_copy(b, d, out_sems.at[q]) for q, (_, b, d) in enumerate(pieces)]
    for load in loads:
        load.start()
    for load, store in zip(loads, stores):
        load.wait()
        store.start()
    for store in stores:
        store.wait()


def shards(genotypes, residual, coefficients, penalty, colors):
    dma = pltpu.SemaphoreType.DMA
    vm = pltpu.VMEM
    coef, res = pl.pallas_call(
        kernel,
        out_shape=(jax.ShapeDtypeStruct((8, 2 * BS), F32), jax.ShapeDtypeStruct((ROWS, K), F32)),
        in_specs=[
            pl.BlockSpec(memory_space=pltpu.SMEM),
            pl.BlockSpec(memory_space=pl.ANY),
            pl.BlockSpec(memory_space=pl.ANY),
            pl.BlockSpec(memory_space=pltpu.VMEM),
            pl.BlockSpec(memory_space=pltpu.VMEM),
        ],
        out_specs=[pl.BlockSpec(memory_space=pl.ANY)] * 2,
        scratch_shapes=[
            vm((2, PAD, BS), BF16), vm((8, 2 * BS), BF16), vm((PAD, K), F32), vm((2, W + 16, PAD), BF16),
            vm((K, W), F32), vm((2, W, BS), F32), vm((W, W), F32),
            vm((2, 2, BS), F32), vm((2, NS, 2, W), F32), vm((2, W), F32), vm((NS, 2, W), F32),
            vm((2, W, W), F32), vm((2, 1, W), F32), vm((2, 1, W), F32), vm((2, 1, BS), F32),
            vm((2, 16, BS), BF16),
            vm((2, 8, BS), F32), vm((2, 8, BS), F32), vm((2, W, W), F32), vm((2, W, W), F32),
            vm((2, W, W), F32), vm((4, 8, BS), F32),
            vm((2, 2, HW, BS), BF16), vm((2, 2, HW, BS), BF16),
            vm((2, 2, NT, HW, W), BF16), vm((2, 2, NT, HW, W), BF16), vm((2, 2, 8, W), F32),
            vm((2, K, BS), BF16),
            vm((2, 2, NV, PR, W), BF16), vm((2, 2, NV, PR, W), BF16), vm((2, 2, NV, PR, W), BF16),
            vm((8, 2 * BS), F32),
            dma((2, 8)), dma, dma, dma((3,)),
            dma, dma, dma, dma, dma, dma, dma((2,)), dma((2,)), dma((2,)), dma((2,)),
            dma((2, 2)), dma((2, 2, 8)), dma((2, 2)), dma((2, 2)), dma((2,)), dma((2,)),
            dma((2, 2)), dma((2, 2, 8)), dma((2, 2)), dma((2, 2)),
            dma((2, 2)), dma((2, 2)), dma((2, 2)), dma((2, 2)),
        ],
        compiler_params=pltpu.CompilerParams(
            collective_id=0, has_side_effects=True, vmem_limit_bytes=56 * 1024 * 1024),
    )(colors.T, genotypes, residual, coefficients, penalty.reshape(2, 1, BS))
    return pl.pallas_call(
        hand_over,
        out_shape=(jax.ShapeDtypeStruct((8, 2 * BS), F32), jax.ShapeDtypeStruct((ROWS, K), F32)),
        in_specs=[pl.BlockSpec(memory_space=pl.ANY)] * 2,
        out_specs=[pl.BlockSpec(memory_space=pl.ANY)] * 2,
        scratch_shapes=[vm((8, 2 * BS), F32), vm((ROWS, K), F32), dma((4,)), dma((4,))],
    )(coef, res)


def solution(mesh):
    placed = (P("samp", "var"), P("samp", None), P("samp", "var"), P("var"), P(None, "var"))
    return jax.shard_map(
        shards,
        mesh=mesh,
        in_specs=placed,
        out_specs=(P("samp", "var"), P("samp", None)),
        check_vma=False,
    )
```

```python
import jax
import jax.numpy as jnp
from jax import lax
from jax.experimental import pallas as pl
from jax.experimental.pallas import tpu as pltpu
from jax.sharding import PartitionSpec as P

K = 256
BS = 2048
ROUNDS = 2
SAMPLES = 34560
ROWS = 1080
PAD = 1152
NS = 32
NT = 16
NV = 8
W = 128
HW = 64
YR = 272
PR = 136
MESH = pl.DeviceIdType.MESH
F32 = jnp.float32
BF16 = jnp.bfloat16
NN_T = (((1,), (1,)), ((), ()))


def al(x, m):
    return pl.multiple_of(x, m)


def zigzag(a, middle):
    return middle + (1 - 2 * (a % 2)) * ((a + 1) // 2)


def split(x):
    high = x.astype(BF16).astype(F32)
    return high, x - high


def kernel(
    colors, x_hbm, res_hbm, coef, pen,
    coef_out, res_out,
    xs, tail, rf, rt, rsum, g, gacc, st_loc, st_in, rg_loc, rg_in, fix, mean_own, scale_own, means, mhl,
    cb, stage, oldr, pick, newb, newt,
    pair_tx, pair_rx, rs_tx, rs_rx, nrm, dmat, c_tx, c_rx, t_buf, cout,
    x_sem, t_sem, r_sem, o_sem,
    st_ss, st_rs, rg_ss, rg_rs, mn_ss, mn_rs, old_ss, old_rs, new_ss, new_rs,
    pr_ss, pr_rs, rs_ss, rs_rs, nm_ss, nm_rs, ag_ss, ag_rs, fw_ss, fw_rs,
    cr_ss, cr_rs, ca_ss, ca_rs,
):
    s = lax.axis_index("samp")
    v = lax.axis_index("var")
    t = s // 2
    c = s % 2
    z = s // 4
    xh = t % 2
    yv = v % 4
    xv = v // 4
    partner = s + 1 - 2 * c
    holder = (s // 8) % 2
    place = pl.ds(al((s // 16) * HW + (s % 8) * 8, 8), 8)
    own_lanes = pl.ds(al(t * W, W), W)

    def chip(i):
        return ((z + zigzag(i // 2, 4)) % 8) * 2 + (xh + 1 - i % 2) % 2

    def group(i):
        return ((xv + 1 - i % 2) % 2) * 4 + (yv + zigzag(i // 2, 2)) % 4

    def rcopy(src, dst, ss, rs, samp, var):
        return pltpu.make_async_remote_copy(
            src_ref=src, dst_ref=dst, send_sem=ss, recv_sem=rs,
            device_id=(samp, var), device_id_type=MESH,
        )

    def arrived(ref, sem):
        rcopy(ref, ref, sem, sem, partner, v).wait_recv()

    def departed(ref, sem):
        rcopy(ref, ref, sem, sem, partner, v).wait_send()

    def chunk(a):
        return pl.ds(al(((z + zigzag(a, 4)) % 8) * 256, 256), 256)

    def x_copy(b, a):
        return pltpu.make_async_copy(
            x_hbm.at[pl.ds(0, 1072), pl.ds(al(b * BS + ((z + zigzag(a, 4)) % 8) * 256, 256), 256)],
            xs.at[b, pl.ds(0, 1072), chunk(a)], x_sem.at[b, a])

    tcopy = pltpu.make_async_copy(x_hbm.at[pl.ds(1072, 8), :], tail, t_sem)
    rcopy_in = pltpu.make_async_copy(res_hbm, rf.at[pl.ds(0, ROWS), :], r_sem)
    rcopy_in.start()
    tcopy.start()

    @pl.loop(0, 8)
    def _(a):
        for b in range(2):
            x_copy(b, a).start()

    coef_copy = pltpu.make_async_copy(cout, coef_out, o_sem.at[2])

    def res_copy(h):
        lanes = pl.ds(h * W, W)
        return pltpu.make_async_copy(rf.at[pl.ds(0, ROWS), lanes], res_out.at[:, lanes], o_sem.at[h])

    barrier = pltpu.get_barrier_semaphore()

    @pl.loop(1, NS)
    def _(i):
        pl.semaphore_signal(barrier, inc=1, device_id=((s + i) % NS, v), device_id_type=MESH)

    @pl.loop(1, NV)
    def _(i):
        pl.semaphore_signal(barrier, inc=1, device_id=(s, (v + i) % NV), device_id_type=MESH)

    for b in range(2):
        cb[b] = coef[:, pl.ds(b * BS, BS)]
        newt[2 + b] = coef[:, pl.ds(b * BS, BS)]
    for r in range(ROUNDS):
        stage[r] = cb[colors[0, r]]

    def transposed(h):
        for i in range(PAD // W):
            rt[h, pl.ds(0, W), pl.ds(i * W, W)] = rf[pl.ds(i * W, W), pl.ds(h * W, W)].T.astype(BF16)
        rsum[pl.ds(h * W, W), :] = jnp.broadcast_to(
            jnp.sum(rt[h, pl.ds(0, W), :].astype(F32), axis=1, keepdims=True), (W, W))

    rf[pl.ds(ROWS, PAD - ROWS), :] = jnp.zeros((PAD - ROWS, K), F32)
    for h in range(2):
        rt[h, pl.ds(W, 16), :] = jnp.ones((16, PAD), BF16)
    for r in range(ROUNDS):
        for h in range(2):
            rs_rx[r, h, t] = jnp.zeros((HW, W), BF16)
            c_rx[r, h, v] = jnp.zeros((PR, W), BF16)
    rcopy_in.wait()
    transposed(0)
    transposed(1)
    for h in range(2):
        rg_loc[pl.ds(h, 1), :] = jnp.sum(
            rf[:, pl.ds(h * W, W)].astype(BF16).astype(F32), axis=0, keepdims=True)
    tcopy.wait()
    for b in range(2):
        xs[b, pl.ds(1088, PAD - 1088), :] = jnp.zeros((PAD - 1088, BS), BF16)
        xs[b, pl.ds(1072, 16), :] = jnp.concatenate(
            [tail[:, pl.ds(b * BS, BS)].astype(F32), jnp.zeros((8, BS), F32)], axis=0).astype(BF16)

    def st_copy(p):
        return rcopy(st_loc.at[:, :, pl.ds(al(p // 2 * W, W), W)], st_in.at[:, s], st_ss, st_rs, p, v)

    def rg_copy(p):
        return rcopy(rg_loc, rg_in.at[s], rg_ss, rg_rs, p, v)

    def old_copy(r, j):
        return rcopy(stage.at[r, :, pl.ds(al(j * W, W), W)], oldr.at[r, place, :],
                     old_ss.at[r], old_rs.at[r], 2 * j + holder, v)

    def old_sends(r):
        @pl.loop(0, NT)
        def _(j):
            @pl.when(2 * j + holder != s)
            def _():
                old_copy(r, j).start()

            @pl.when(2 * j + holder == s)
            def _():
                oldr[r, place, :] = stage[r, :, pl.ds(al(j * W, W), W)]

    def each(wait, some, every):
        @pl.when(holder == c)
        def _():
            wait(some)

        @pl.when(holder != c)
        def _():
            wait(every)

    def old_drain(r):
        each(lambda ref: departed(ref, old_ss.at[r]), oldr.at[r, pl.ds(0, W - 8), :], oldr.at[r])

    def sharer(i):
        return (i // 8) * 16 + c * 8 + i % 8

    def old_wait(r):
        each(lambda ref: arrived(ref, old_rs.at[r]), oldr.at[r, pl.ds(0, W - 8), :], oldr.at[r])

    def new_copy(r, i):
        return rcopy(newb.at[r, pl.ds(al(i * 8, 8), 8), :], newt.at[r, :, own_lanes],
                     new_ss.at[r], new_rs.at[r], sharer(i), v)

    def new_wait(r):
        each(lambda ref: arrived(ref, new_rs.at[r]), newt.at[r, :, pl.ds(0, BS - W)], newt.at[r])

    def new_drain(r):
        each(lambda ref: departed(ref, new_ss.at[r]), newb.at[r, pl.ds(0, W - 8), :], newb.at[r])

    def ca_copy(r, h, p):
        return rcopy(t_buf.at[r, h, v], t_buf.at[r, h, v], ca_ss.at[r, h], ca_rs.at[r, h], s, p)

    def ca_drain(r, h):
        departed(t_buf.at[r, h, pl.ds(0, NV - 1)], ca_ss.at[r, h])

    def own_rows(h):
        return pl.ds(al(c * HW, HW), HW)

    def pair_copy(r, h, a):
        return rcopy(pair_tx.at[r, h, :, chunk(a)], pair_rx.at[r, h, :, chunk(a)],
                     pr_ss.at[r, h], pr_rs.at[r, h, a], partner, v)

    def moments(a):
        lanes = chunk(a)

        @pl.loop(0, 2)
        def _(b):
            cnt = jnp.zeros((16, 256), F32)
            sqr = jnp.zeros((16, 256), F32)
            for e in range(2):
                x = xs[b, pl.ds(e * 576, 16), lanes]
                one = x
                two = x * x
                for i in range(1, 36):
                    x = xs[b, pl.ds(e * 576 + i * 16, 16), lanes]
                    one = one + x
                    two = two + x * x
                cnt = cnt + one.astype(F32)
                sqr = sqr + two.astype(F32)
            st_loc[b, pl.ds(0, 1), lanes] = jnp.sum(cnt, axis=0, keepdims=True)
            st_loc[b, pl.ds(1, 1), lanes] = jnp.sum(sqr, axis=0, keepdims=True)

    def product(r, h, a, send=True):
        lanes = chunk(a)
        if r == 0:
            out = jnp.dot(rt[h], xs[colors[0, r], :, lanes], preferred_element_type=F32)
            mean = out[W:W + 1] * (1.0 / ROWS)
            out = out[:W]
        else:
            out = jnp.dot(rt[h, pl.ds(0, W), :], xs[colors[0, r], :, lanes], preferred_element_type=F32)
            mean = means[colors[0, r], :, lanes]
        g[h, :, lanes] = out - rsum[pl.ds(h * W, W), :][:, 0:1] * mean
        pair_tx[r, h, :, lanes] = g[h, pl.ds(al((1 - c) * HW, HW), HW), lanes].astype(BF16)
        if send:
            pair_copy(r, h, a).start()

    def rs_copy(r, h, j):
        return rcopy(rs_tx.at[r, h, j], rs_rx.at[r, h, t], rs_ss.at[r, h], rs_rs.at[r, h], 2 * j + c, v)

    def send_on(r, h, a):
        lanes = chunk(a)
        pair_copy(r, h, a).wait_recv()
        mine = g[h, own_rows(h), lanes] + pair_rx[r, h, :, lanes].astype(F32)
        g[h, own_rows(h), lanes] = mine
        low = mine.astype(BF16)
        for e in range(2):
            j = ((z + zigzag(a, 4)) % 8) * 2 + e
            rs_tx[r, h, j] = low[:, e * W:(e + 1) * W]

            @pl.when(j != t)
            def _():
                rs_copy(r, h, j).start()

    def gradient(r, h):
        @pl.loop(0, 3)
        def _(a):
            product(r, h, a, send=r + h > 0)

        if r + h == 0:
            pl.semaphore_wait(barrier, NS - 1 + NV - 1)

            @pl.loop(0, 3)
            def _(a):
                pair_copy(0, 0, a).start()

            @pl.loop(1, NS)
            def _(i):
                rg_copy((s + i) % NS).start()

            rg_in[s] = rg_loc[...]
            old_sends(0)

        @pl.loop(3, 8)
        def _(a):
            product(r, h, a)
            send_on(r, h, a - 3)

        @pl.loop(5, 8)
        def _(a):
            send_on(r, h, a)

    @pl.loop(0, 8)
    def _(a):
        for b in range(2):
            x_copy(b, a).wait()
        moments(a)

    gradient(0, 0)

    @pl.loop(1, NS)
    def _(i):
        st_copy((s + i) % NS).start()

    st_in[:, s] = st_loc[:, :, own_lanes]
    gradient(0, 1)

    def mn_copy(j):
        return rcopy(mean_own, means.at[:, :, own_lanes], mn_ss, mn_rs, 2 * j + c, v)

    st_all = st_in.at[:, pl.ds(0, NS - 1)]
    rg_all = rg_in.at[pl.ds(0, NS - 1)]
    mn_all = means.at[:, :, pl.ds(0, (NT - 1) * W)]

    def statistics():
        arrived(st_all, st_rs)
        arrived(rg_all, rg_rs)

        for b in range(2):
            total = jnp.sum(st_in[b], axis=0)
            mean = total[0:1] / SAMPLES
            mean_own[b] = mean
            means[b, :, own_lanes] = mean
            scale_own[b] = total[1:2] - total[0:1] * mean

        @pl.loop(0, NT - 1)
        def _(i):
            mn_copy(chip(i)).start()

        b_high, b_low = split(st_in[colors[0, 0]][:, 0, :] * (1.0 / ROWS) - mean_own[colors[0, 0]])
        right = jnp.concatenate([b_high, b_low, b_high, b_low], axis=0).astype(BF16)
        for h in range(2):
            a_high, a_low = split(rg_in[:, h, :])
            left = jnp.concatenate([a_high, a_high, a_low, a_low], axis=0)
            fix[h] = jnp.dot(left.T.astype(BF16), right, preferred_element_type=F32)
            gacc[pl.ds(h * HW, HW), :] = gacc[pl.ds(h * HW, HW), :] + fix[h, own_rows(h), :]

    def d_view(r, h, core, j):
        return dmat.at[r, pl.ds(al(h * W + core * HW, HW), HW), pl.ds(al(j * W, W), W)]

    def ag_copy(r, h, j):
        own = d_view(r, h, c, t)
        return rcopy(own, own, ag_ss.at[r, h], ag_rs.at[r, h, z], 2 * j + c, v)

    def level(r, h, k):
        return dmat.at[r, pl.ds(al(h * W + c * HW, HW), HW), pl.ds(al(k * 256, 256), 256)]

    def fw_copy(r, h, k):
        return rcopy(level(r, h, k), level(r, h, k), fw_ss.at[r, h], fw_rs.at[r, h], partner, v)

    def cr_copy(r, h, p):
        return rcopy(c_tx.at[r, h, p], c_rx.at[r, h, v], cr_ss.at[r, h], cr_rs.at[r, h], s, p)

    def ag_drain(r):
        for h in range(2):
            departed(dmat.at[r, pl.ds(0, HW), pl.ds(0, (NT - 1) * W)], ag_ss.at[r, h])
            departed(dmat.at[r, pl.ds(0, HW), :], fw_ss.at[r, h])

    def cr_drain(r):
        for h in range(2):
            departed(c_tx.at[r, h, pl.ds(0, NV - 1)], cr_ss.at[r, h])

    for r in range(ROUNDS):
        color = colors[0, r]

        if r == 1:
            ag_drain(0)
            cr_drain(0)

        for h in range(2):
            rows = pl.ds(h * HW, HW)
            arrived(rs_rx.at[r, h, pl.ds(0, NT - 1)], rs_rs.at[r, h])
            total = g[h, own_rows(h), own_lanes]
            for j in range(NT):
                total = total + rs_rx[r, h, j].astype(F32)
            gacc[rows, :] = total

        old_wait(r)
        if r == 0:
            statistics()
            old = oldr[0]
        else:
            pick[0] = oldr[1]
            gap = color - colors[0, 0]
            old = pick[1 - gap * gap]
        scale = scale_own[color]
        shifted = old + gacc[...] / scale
        part = jnp.sum(shifted * shifted, axis=0, keepdims=True)
        nrm[r, 0] = jnp.broadcast_to(part, (8, W))
        ncopy = rcopy(nrm.at[r, 0], nrm.at[r, 1], nm_ss.at[r], nm_rs.at[r], partner, v)
        ncopy.start()
        push = pen[color, :, own_lanes] * jnp.sqrt(K / scale)
        ncopy.wait_recv()
        norm = jnp.sqrt(part + nrm[r, 1][0:1] + 1e-06)
        new = jnp.maximum(0.0, 1.0 - push / norm) * shifted
        change = (new - old).astype(BF16)
        for h in range(2):
            dmat[r, pl.ds(al(h * W + c * HW, HW), HW), own_lanes] = change[h * HW:(h + 1) * HW]
        newb[r] = new
        if r == 0:
            pick[1] = new

        for h in range(2):
            @pl.loop(0, NT - 1)
            def _(i):
                ag_copy(r, h, chip(i)).start()


        if r == 0:
            departed(st_all, st_ss)
            departed(rg_all, rg_ss)
            departed(mn_all, mn_ss)
            old_drain(0)
            arrived(mn_all, mn_rs)
            for b in range(2):
                high, low = split(means[b])
                mhl[b] = jnp.concatenate(
                    [jnp.broadcast_to(high, (8, BS)), jnp.broadcast_to(low, (8, BS))], axis=0).astype(BF16)
        else:
            old_drain(1)
            new_drain(0)
            ca_drain(0, 0)
            ca_drain(0, 1)
        ncopy.wait_send()
        for h in range(2):
            departed(pair_tx.at[r, h], pr_ss.at[r, h])
            departed(rs_tx.at[r, h, pl.ds(0, NT - 1)], rs_ss.at[r, h])

        for h in range(2):
            @pl.loop(0, 7)
            def _(a):
                k = (z + zigzag(a, 4)) % 8
                arrived(level(r, h, k), ag_rs.at[r, h, k])
                fw_copy(r, h, k).start()

            arrived(d_view(r, h, c, t + 1 - 2 * xh), ag_rs.at[r, h, z])
            fw_copy(r, h, z).start()

            arrived(dmat.at[r, pl.ds(0, HW), :], fw_rs.at[r, h])

            rows = pl.ds(h * W, W)
            md = lax.dot_general(mhl[color], dmat[r, rows, :], NN_T, preferred_element_type=F32)
            md = md[0:1] + md[8:9]

            @pl.loop(0, 4)
            def _(i):
                y = (yv + zigzag(i, 2)) % 4
                out = lax.dot_general(xs[color, pl.ds(al(y * YR, 16), YR), :], dmat[r, rows, :], NN_T,
                                      preferred_element_type=F32) - md
                for w in range(2):
                    c_tx[r, h, w * 4 + y] = out[w * PR:(w + 1) * PR].astype(BF16)
                for w in range(2):
                    p = w * 4 + y

                    @pl.when(p != v)
                    def _():
                        cr_copy(r, h, p).start()

        def add_up(h):
            arrived(c_rx.at[r, h, pl.ds(0, NV - 1)], cr_rs.at[r, h])
            total = c_tx[r, h, v].astype(F32)
            for p in range(NV):
                total = total + c_rx[r, h, p].astype(F32)
            t_buf[r, h, v] = total.astype(BF16)

            @pl.loop(0, NV - 1)
            def _(i):
                ca_copy(r, h, group(i)).start()

        add_up(0)

        @pl.loop(0, 16)
        def _(i):
            @pl.when(sharer(i) != s)
            def _():
                new_copy(r, i).start()

            @pl.when(sharer(i) == s)
            def _():
                newt[r, :, own_lanes] = newb[r, pl.ds(al(i * 8, 8), 8), :]

        if r == 0:
            old_sends(1)
        else:
            ag_drain(1)

        add_up(1)

        if r == 1:
            cr_drain(r)

        if r == 1:
            new_wait(0)
            new_wait(1)

            for b in range(2):
                d0 = colors[0, 0] - b
                d1 = colors[0, 1] - b
                cout[:, pl.ds(b * BS, BS)] = newt[1 - d1 * d1 + d1 * d1 * d0 * d0 * (2 + b)]
            coef_copy.start()
            new_drain(r)

        for h in range(2):
            lanes = pl.ds(h * W, W)

            arrived(t_buf.at[r, h, pl.ds(0, NV - 1)], ca_rs.at[r, h])
            for p in range(NV):
                rows = pl.ds((p % 4) * YR + (p // 4) * PR, PR)
                rf[rows, lanes] = rf[rows, lanes] - t_buf[r, h, p].astype(F32)

            if r == 0:
                rf[pl.ds(ROWS, 8), lanes] = jnp.zeros((8, W), F32)
                transposed(h)
                gradient(1, h)
            else:
                res_copy(h).start()

    ca_drain(1, 0)
    ca_drain(1, 1)
    coef_copy.wait()
    res_copy(0).wait()
    res_copy(1).wait()


def hand_over(coef, res, coef_out, res_out, coef_vmem, res_vmem, in_sems, out_sems):
    pieces = [(coef, coef_vmem, coef_out)]
    for q in range(3):
        rows = pl.ds(q * 360, 360)
        pieces.append((res.at[rows, :], res_vmem.at[rows, :], res_out.at[rows, :]))
    loads = [pltpu.make_async_copy(a, b, in_sems.at[q]) for q, (a, b, _) in enumerate(pieces)]
    stores = [pltpu.make_async_copy(b, d, out_sems.at[q]) for q, (_, b, d) in enumerate(pieces)]
    for load in loads:
        load.start()
    for load, store in zip(loads, stores):
        load.wait()
        store.start()
    for store in stores:
        store.wait()


def shards(genotypes, residual, coefficients, penalty, colors):
    dma = pltpu.SemaphoreType.DMA
    vm = pltpu.VMEM
    coef, res = pl.pallas_call(
        kernel,
        out_shape=(jax.ShapeDtypeStruct((8, 2 * BS), F32), jax.ShapeDtypeStruct((ROWS, K), F32)),
        in_specs=[
            pl.BlockSpec(memory_space=pltpu.SMEM),
            pl.BlockSpec(memory_space=pl.ANY),
            pl.BlockSpec(memory_space=pl.ANY),
            pl.BlockSpec(memory_space=pltpu.VMEM),
            pl.BlockSpec(memory_space=pltpu.VMEM),
        ],
        out_specs=[pl.BlockSpec(memory_space=pl.ANY)] * 2,
        scratch_shapes=[
            vm((2, PAD, BS), BF16), vm((8, 2 * BS), BF16), vm((PAD, K), F32), vm((2, W + 16, PAD), BF16),
            vm((K, W), F32), vm((2, W, BS), F32), vm((W, W), F32),
            vm((2, 2, BS), F32), vm((2, NS, 2, W), F32), vm((2, W), F32), vm((NS, 2, W), F32),
            vm((2, W, W), F32), vm((2, 1, W), F32), vm((2, 1, W), F32), vm((2, 1, BS), F32),
            vm((2, 16, BS), BF16),
            vm((2, 8, BS), F32), vm((2, 8, BS), F32), vm((2, W, W), F32), vm((2, W, W), F32),
            vm((2, W, W), F32), vm((4, 8, BS), F32),
            vm((2, 2, HW, BS), BF16), vm((2, 2, HW, BS), BF16),
            vm((2, 2, NT, HW, W), BF16), vm((2, 2, NT, HW, W), BF16), vm((2, 2, 8, W), F32),
            vm((2, K, BS), BF16),
            vm((2, 2, NV, PR, W), BF16), vm((2, 2, NV, PR, W), BF16), vm((2, 2, NV, PR, W), BF16),
            vm((8, 2 * BS), F32),
            dma((2, 8)), dma, dma, dma((3,)),
            dma, dma, dma, dma, dma, dma, dma((2,)), dma((2,)), dma((2,)), dma((2,)),
            dma((2, 2)), dma((2, 2, 8)), dma((2, 2)), dma((2, 2)), dma((2,)), dma((2,)),
            dma((2, 2)), dma((2, 2, 8)), dma((2, 2)), dma((2, 2)),
            dma((2, 2)), dma((2, 2)), dma((2, 2)), dma((2, 2)),
        ],
        compiler_params=pltpu.CompilerParams(
            collective_id=0, has_side_effects=True, vmem_limit_bytes=56 * 1024 * 1024),
    )(colors.T, genotypes, residual, coefficients, penalty.reshape(2, 1, BS))
    return pl.pallas_call(
        hand_over,
        out_shape=(jax.ShapeDtypeStruct((8, 2 * BS), F32), jax.ShapeDtypeStruct((ROWS, K), F32)),
        in_specs=[pl.BlockSpec(memory_space=pl.ANY)] * 2,
        out_specs=[pl.BlockSpec(memory_space=pl.ANY)] * 2,
        scratch_shapes=[vm((8, 2 * BS), F32), vm((ROWS, K), F32), dma((4,)), dma((4,))],
    )(coef, res)


def solution(mesh):
    placed = (P("samp", "var"), P("samp", None), P("samp", "var"), P("var"), P(None, "var"))
    return jax.shard_map(
        shards,
        mesh=mesh,
        in_specs=placed,
        out_specs=(P("samp", "var"), P("samp", None)),
        check_vma=False,
    )
```
